256 devices in a mesh: dp: 16 (over z, x_lo), seq: 16 (over y, x_hi, core).
Axes of the slice: x: 4 (x_hi: 2, x_lo: 2; x = x_hi * 2 + x_lo), y: 4, z: 8, core: 2. Of those that a mesh axis runs over, the one named last changes fastest.
Arguments:
- frames: bfloat16 [16, 4096, 1536], P('dp', 'seq'), may hold values from -0.29882812 to 0.29882812
- segment_ids: int32 [16, 4096], P('dp', 'seq'), may hold values from 0 to 11, never falling along the last dimension, each value on 1 to 3072 neighbouring positions
- ln_attn_gain: float32 [1536], replicated, may hold values from 0.25 to 1.75
- w_qkv: bfloat16 [1536, 2304], P('dp'), as said below
- w_out: bfloat16 [768, 1536], P('dp'), may hold values from -0.21875 to 0.21875
- ln_conv_gain: float32 [1536], replicated, may hold values from 0.25 to 1.75
- w_glu: bfloat16 [1536, 3072], P('dp'), may hold values from -0.15625 to 0.15625
- dw_kernel: float32 [32, 1536], replicated, may hold values from -1 to 1
- ln_mid_gain: float32 [1536], replicated, may hold values from 0.25 to 1.75
Outputs:
- block_out: bfloat16 [16, 4096, 1536], P('dp', 'seq')
The draws below stay inside these ranges and needn't reach their ends.
Inputs may be any that keep to these rules, and one draw needn't show every extreme that they name: `segment_ids`: within each stream the ids start at 0 and never fall; each utterance has 1 to 3072 frames and one has exactly 3072. `w_qkv`: a projection matrix with independent entries.
All inputs are finite; a program needn't handle non-finite values.
Results may differ from the reference program's by a relative error of at most 0.025.
The reference program's roundings to bfloat16 on the way (of `normed`, `projected`, `weights`, `attended`, `resid` and `gated`) count: a program that leaves them out, or rounds other values in their place, can miss the bound.
Values may be sent and summed in bfloat16 or wider, within the bound.
No kernel may reach another device: no remote copies, remote signals or barrier semaphores. Data moves between devices by JAX's collectives and lax.ppermute only.
A program may use at most 192 MiB of HBM per device.

```python
import math
import jax
import jax.numpy as jnp
import numpy as np
from jax import lax

D = 1536
HEADS = 12
HD = 64
CONV_K = 32
SEGS = 12
LEN = 4096
STREAMS = 16
SEG_MOST = 3072


def draw_w_qkv(key, part):
    width = HEADS * HD
    matrix = jax.random.normal(key, (D, 3 * width), jnp.float32) * D ** (-0.5)
    return matrix.astype(jnp.bfloat16)


def levels(key, dims, cuts, low, top_value):
    level, own = 1.0, jax.random.fold_in(key, 6)
    for position, blocks in cuts:
        steps = jnp.exp(jax.random.uniform(jax.random.fold_in(own, position), (blocks,), jnp.float32, low / len(cuts), top_value / len(cuts)))
        level = level * jnp.repeat(steps, dims[position] // blocks).reshape([-1 if axis == position else 1 for axis in range(len(dims))])
    return level


def length_profile(amount, total, limit, lean):
    weights = [(1 << 20) // math.isqrt(rank ** lean) + 1 for rank in range(2, amount + 1)]
    rest, counts = total - limit - (amount - 1), [1] * (amount - 1)
    while rest > 0:
        free = [i for i in range(amount - 1) if counts[i] < limit]
        whole, remaining = sum([weights[i] for i in free]), rest
        for i in free:
            extra = min(limit - counts[i], max(1, remaining * weights[i] // whole), rest)
            counts[i] = counts[i] + extra
            rest = rest - extra
    return np.array([limit] + counts)


def uneven_parts(own_key, amount, total, reach, skew):
    if amount == 2:
        one = jax.random.randint(own_key, (), max(1, total - reach), min(reach, total - 1) + 1)
        return jnp.stack([one, total - one])
    sizes = jnp.asarray(length_profile(amount, total, reach, skew), jnp.int32)
    twos = (amount - 1) // 2
    donor, sink = sizes[1:1 + 2 * twos:2], sizes[2:2 + 2 * twos:2]
    slack = jnp.minimum(donor - 1, reach - sink)
    passed = jax.random.randint(jax.random.fold_in(own_key, 1), (twos,), 0, 1 << 20) % (slack + 1)
    sizes = sizes.at[1:1 + 2 * twos:2].set(donor - passed).at[2:2 + 2 * twos:2].set(sink + passed)
    return sizes[jax.random.permutation(jax.random.fold_in(own_key, 2), amount)]


def bell_draw(rng, extent, deviation, limit, pieces=(), dtype=jnp.bfloat16):
    level = levels(rng, extent, pieces, -0.22, 0.18) if pieces else 1.0
    entries = jax.random.normal(rng, extent, jnp.float32) * deviation * level
    return jnp.minimum(jnp.maximum(entries, -limit), limit).astype(dtype)


def setup_inputs(seed: int = 0) -> dict:
    streams_of = jax.random.split(jax.random.key(seed), 10)
    frames = bell_draw(streams_of[0], (STREAMS, LEN, D), 0.05, 0.29882812, ((0, 16), (1, 16)))
    segment_ids = jax.vmap(lambda own: jnp.searchsorted(jnp.cumsum(uneven_parts(own, SEGS, LEN, SEG_MOST, 2)), jnp.arange(LEN), side="right"))(jax.random.split(streams_of[1], STREAMS)).reshape((STREAMS, LEN)).astype(jnp.int32)
    ln_attn_gain = jnp.clip(1.0 + 0.15 * jax.random.normal(streams_of[2], (D,), jnp.float32), 0.25, 1.75)
    w_qkv = draw_w_qkv(jax.random.fold_in(streams_of[9], 71), 0)
    w_out = bell_draw(streams_of[4], (HEADS * HD, D), (HEADS * HD) ** -0.5, 0.21875, ((0, 16),))
    ln_conv_gain = jnp.clip(1.0 + 0.15 * jax.random.normal(streams_of[5], (D,), jnp.float32), 0.25, 1.75)
    w_glu = bell_draw(streams_of[6], (D, 2 * D), D ** -0.5, 0.15625, ((0, 16),))
    dw_kernel = bell_draw(streams_of[7], (CONV_K, D), CONV_K ** -0.5, 1.0, (), jnp.float32)
    ln_mid_gain = jnp.clip(1.0 + 0.15 * jax.random.normal(streams_of[8], (D,), jnp.float32), 0.25, 1.75)
    return dict(frames=frames, segment_ids=segment_ids, ln_attn_gain=ln_attn_gain, w_qkv=w_qkv, w_out=w_out, ln_conv_gain=ln_conv_gain, w_glu=w_glu, dw_kernel=dw_kernel, ln_mid_gain=ln_mid_gain)


def layer_norm(values, gain):
    values = values.astype(jnp.float32)
    centre = lax.optimization_barrier(jnp.mean(values, -1, keepdims=True))
    spread = lax.optimization_barrier(jnp.mean((values - centre) ** 2, -1, keepdims=True))
    return (values - centre) * lax.rsqrt(spread + 1e-05) * gain

def reference(frames, segment_ids, ln_attn_gain, w_qkv, w_out, ln_conv_gain, w_glu, dw_kernel, ln_mid_gain):
    width = HEADS * HD
    block_rows = math.gcd(LEN, 512)

    def one_stream(pair):
        stream, segments = pair
        normed = layer_norm(stream, ln_attn_gain).astype(jnp.bfloat16)
        projected = jnp.dot(normed, w_qkv, preferred_element_type=jnp.float32).astype(jnp.bfloat16)
        queries = projected[:, :width].astype(jnp.float32).reshape(LEN, HEADS, HD)
        keys_all = projected[:, width:2 * width].astype(jnp.float32).reshape(LEN, HEADS, HD)
        values_all = projected[:, 2 * width:].astype(jnp.float32).reshape(LEN, HEADS, HD)

        def attend(block_start):
            query_blk = lax.dynamic_slice_in_dim(queries, block_start, block_rows)
            query_segs = lax.dynamic_slice_in_dim(segments, block_start, block_rows)
            scores = jnp.einsum('qhd,khd->hqk', query_blk, keys_all, precision=lax.Precision.HIGHEST) / math.sqrt(HD)
            same_seg = (query_segs[:, None] == segments[None, :])[None]
            scores = jnp.where(same_seg, scores, -1e+30)
            highest = lax.optimization_barrier(jnp.max(scores, -1, keepdims=True))
            raised = jnp.where(same_seg, jnp.exp(scores - highest), 0.0)
            totals = lax.optimization_barrier(jnp.sum(raised, -1))
            rounded = raised.astype(jnp.bfloat16).astype(jnp.float32)
            mixed = jnp.einsum('hqk,khd->qhd', rounded, values_all, precision=lax.Precision.HIGHEST)
            mixed = mixed / jnp.transpose(totals)[:, :, None]
            return mixed.reshape(block_rows, width).astype(jnp.bfloat16)
        starts = (jnp.arange(LEN // block_rows) * block_rows).astype(jnp.int32)
        attended = lax.map(attend, starts).reshape(LEN, width)
        attn = jnp.dot(attended, w_out, preferred_element_type=jnp.float32)
        resid = (stream.astype(jnp.float32) + attn).astype(jnp.bfloat16)
        glu_in = layer_norm(resid, ln_conv_gain).astype(jnp.bfloat16)
        glu_out = jnp.dot(glu_in, w_glu, preferred_element_type=jnp.float32)
        gated = (glu_out[:, :D] * jax.nn.sigmoid(glu_out[:, D:])).astype(jnp.bfloat16)
        half_taps = CONV_K // 2
        padded = jnp.pad(gated.astype(jnp.float32), ((half_taps, half_taps), (0, 0)))
        padded_segs = jnp.pad(segments, (half_taps, half_taps), constant_values=-1)
        conv = jnp.zeros((LEN, D), jnp.float32)
        for tap_index in range(CONV_K):
            keep = (padded_segs[tap_index:tap_index + LEN] == segments)[:, None]
            conv = conv + jnp.where(keep, padded[tap_index:tap_index + LEN] * dw_kernel[tap_index], 0.0)
        middle = layer_norm(conv, ln_mid_gain)
        return (resid.astype(jnp.float32) + middle * jax.nn.sigmoid(middle)).astype(jnp.bfloat16)
    return lax.map(one_stream, (frames, segment_ids))
```

```python
import functools

import jax
import jax.numpy as jnp
from jax import lax
from jax.experimental import pallas as pl
from jax.experimental.pallas import tpu as pltpu
from jax.sharding import Mesh
from jax.sharding import PartitionSpec as P

D = 1536
HEADS = 12
HD = 64
CONV_K = 32
HALF = CONV_K // 2
WIDTH = HEADS * HD
ROWS = 256
GROUP = 4
CHUNK = GROUP * ROWS
HCOLS = WIDTH // GROUP
LEN = 4096
KB = 512
QT = 256
NEG = -1e30
F32, BF16 = jnp.float32, jnp.bfloat16
ANY = pl.BlockSpec(memory_space=pl.ANY)
VM = pl.BlockSpec(memory_space=pltpu.VMEM)
SM = pl.BlockSpec(memory_space=pltpu.SMEM)


def params(limit_mib=40):
    return pltpu.CompilerParams(vmem_limit_bytes=limit_mib << 20)


def cost(us):
    return pl.CostEstimate(flops=int(us * 9e8), bytes_accessed=int(us * 2e6), transcendentals=0)


def shift(value, axis, count, step):
    return lax.ppermute(value, axis, [(i, (i + step) % count) for i in range(count)])


def swap(value, axes, mask, count):
    return lax.ppermute(value, axes, [(i, i ^ mask) for i in range(count)])


def z_ring(buf, cut):
    f, b = [buf], [buf]
    for _ in range(3):
        f.append(shift(f[-1], "z", 8, 1))
        b.append(shift(b[-1], "z", 8, -1))
    h0 = shift(f[3][:cut], "z", 8, 1)
    h1 = shift(b[3][cut:], "z", 8, -1)
    return f, b, h0, h1


def norm(values, gain):
    centre = jnp.mean(values, -1, keepdims=True)
    shifted = values - centre
    spread = jnp.mean(shifted * shifted, -1, keepdims=True)
    return shifted * lax.rsqrt(spread + 1e-05) * gain


def qkv_kernel(n0, n1, n2, n3, p0, f1, f2, f3, b1, b2, b3, h0, h1, kv_ref, q_ref, w, sem):
    z, xl = lax.axis_index("z"), lax.axis_index("xl")
    me = lax.axis_index("xh") * 2 + lax.axis_index("c")

    def place(src, zz, half, own):
        owner = lax.rem(zz + 8, 8) * 2 + (xl if own else 1 - xl)
        rows = pl.ds(pl.multiple_of(owner * 96, 96), 96)
        return pltpu.make_async_copy(src.at[pl.ds(half * 96, 96)], w.at[rows], sem)

    copies = []
    for ref, off in ((p0, 0), (f1, -1), (f2, -2), (f3, -3), (b1, 1), (b2, 2), (b3, 3)):
        copies.append(place(ref, z + off, 0, True))
        copies.append(place(ref, z + off, 1, False))
    copies.append(place(h0, z + 4, 0, True))
    copies.append(place(h1, z + 4, 0, False))
    for cp in copies:
        cp.start()
    for cp in copies:
        cp.wait()
    for r, ref in enumerate((n0, n1, n2, n3)):
        rows = pl.ds(pl.multiple_of((me ^ r) * ROWS, ROWS), ROWS)
        out = jnp.dot(ref[...], w[...], preferred_element_type=F32).astype(BF16)
        kv_ref[rows, :] = out[:, :384]
        q_ref[rows, :] = out[:, 384:]


def qkv(normed, ring):
    f, b, h0, h1 = ring
    return pl.pallas_call(
        qkv_kernel,
        name="qkv",
        out_shape=(
            jax.ShapeDtypeStruct((CHUNK, 384), BF16),
            jax.ShapeDtypeStruct((CHUNK, 256), BF16),
        ),
        in_specs=[VM] * 4 + [ANY] * 9,
        out_specs=(VM, VM),
        scratch_shapes=[pltpu.VMEM((D, 640), BF16), pltpu.SemaphoreType.DMA],
        compiler_params=params(),
        cost_estimate=cost(5),
    )(*normed, f[0], *f[1:], *b[1:], h0, h1)


def attn_kernel(parts, first, last, lo_ref, hi_ref, q_ref, qseg_ref, kseg_ref, *refs):
    kvs, refs = refs[: len(parts)], refs[len(parts) :]
    if first:
        outs, (qs, m, l, acc) = refs[:-4], refs[-4:]
    else:
        (ml_in, acc_in), outs, (qs, m, l, acc) = refs[:2], refs[2:-4], refs[-4:]
    y = lax.axis_index("y")
    tile = pl.program_id(0)
    lane = lax.broadcasted_iota(jnp.int32, (QT, 128), 1)
    low = lane < HD
    qa, qb = q_ref[:, :128] * BF16(0.125), q_ref[:, 128:] * BF16(0.125)
    zero = jnp.zeros_like(qa)
    qs[0] = jnp.where(low, qa, zero)
    qs[1] = jnp.where(low, zero, qa)
    qs[2] = qb
    if first:
        m[...] = jnp.full_like(m, NEG)
        l[...] = jnp.zeros_like(l)
        acc[...] = jnp.zeros_like(acc)
    else:
        for h in range(3):
            m[h] = jnp.broadcast_to(ml_in[:, h : h + 1], (QT, 128))
            l[h] = jnp.broadcast_to(ml_in[:, 3 + h : 4 + h], (QT, 128))
        acc[0] = acc_in[:, :128]
        acc[1] = acc_in[:, 128:256]
        acc[2] = acc_in[:, 256:]
    qblk = y * GROUP + tile
    qlo, qhi = lo_ref[qblk], hi_ref[qblk]

    def step(kv, row, kseg, masked):
        if masked:
            same = qseg_ref[:, :1] == kseg_ref[pl.ds(kseg, 1), :]
        for h in range(3):
            keys = kv[pl.ds(row, KB), :128] if h < 2 else kv[pl.ds(row, KB), 128:256]
            vals = kv[pl.ds(row, KB), 256:] if h < 2 else keys
            s = lax.dot_general(
                qs[h], keys, (((1,), (1,)), ((), ())), preferred_element_type=F32
            )
            if masked:
                s = jnp.where(same, s, NEG)
            old = m[h]
            new = jnp.maximum(old, jnp.max(s, axis=1, keepdims=True))
            p = jnp.exp(s - new[:, :1])
            alpha = jnp.exp(old - new)
            m[h] = new
            l[h] = alpha * l[h] + jnp.sum(p, axis=1, keepdims=True)
            pv = jnp.dot(p.astype(BF16), vals, preferred_element_type=F32)
            acc[h] = alpha * acc[h] + pv

    for kv, (off, start, count) in zip(kvs, parts):
        chunk = lax.rem(y + off + 4, 4)

        @pl.loop(0, count // KB)
        def _(i):
            kseg = chunk * (CHUNK // KB) + start // KB + i
            klo, khi = lo_ref[kseg * 2], hi_ref[kseg * 2 + 1]
            row = pl.multiple_of(i * KB, KB)
            meet = jnp.logical_and(klo <= qhi, qlo <= khi)
            plain = jnp.logical_and(jnp.logical_and(klo == khi, qlo == qhi), klo == qlo)

            @pl.when(plain)
            def _():
                step(kv, row, kseg, False)

            @pl.when(jnp.logical_and(meet, jnp.logical_not(plain)))
            def _():
                step(kv, row, kseg, True)

    if last:
        (out,) = outs
        o01 = jnp.where(low, acc[0] / l[0], acc[1] / l[1])
        out[:, :128] = o01.astype(BF16)
        out[:, 128:] = jnp.where(low, acc[2] / l[2], 0.0).astype(BF16)
    else:
        ml_out, acc_out = outs
        packed = jnp.zeros((QT, 128), F32)
        for h in range(3):
            packed = jnp.where(lane == h, m[h], packed)
            packed = jnp.where(lane == 3 + h, l[h], packed)
            acc_out[:, h * 128 : (h + 1) * 128] = acc[h]
        ml_out[...] = packed


def attend(parts, q, qseg, kseg, lo, hi, kvs, state, last, us):
    first = state is None
    tiles = CHUNK // QT

    def rows(cols):
        return pl.BlockSpec((QT, cols), lambda i: (i, 0))

    state_shapes = (
        jax.ShapeDtypeStruct((CHUNK, 128), F32),
        jax.ShapeDtypeStruct((CHUNK, 384), F32),
    )
    return pl.pallas_call(
        functools.partial(attn_kernel, parts, first, last),
        name="attend",
        grid=(tiles,),
        out_shape=jax.ShapeDtypeStruct((CHUNK, 256), BF16) if last else state_shapes,
        in_specs=[SM, SM, rows(256), rows(128), VM]
        + [VM] * len(kvs)
        + ([] if first else [rows(128), rows(384)]),
        out_specs=rows(256) if last else (rows(128), rows(384)),
        scratch_shapes=[
            pltpu.VMEM((3, QT, 128), BF16),
            pltpu.VMEM((3, QT, 128), F32),
            pltpu.VMEM((3, QT, 128), F32),
            pltpu.VMEM((3, QT, 128), F32),
        ],
        compiler_params=params(),
        cost_estimate=cost(us),
    )(lo, hi, q, qseg, kseg, *kvs, *(() if first else state))


def glu_kernel(a0, a1, a2, a3, local, gain, *refs):
    srcs, (resid_ref, gated_ref, wo, wv, wg, sem_o, sem_g) = refs[:18], refs[18:]
    z, c = lax.axis_index("z"), lax.axis_index("c")
    me = lax.axis_index("xh") * 2 + c
    out_copies, glu_copies = [], []

    def rows(owner, count):
        return pl.ds(pl.multiple_of(owner * count, count), count)

    for k in range(2):
        own = c if k == 0 else 1 - c
        p0, f1, f2, f3, b1, b2, b3, h0, h1 = srcs[9 * k : 9 * k + 9]
        whole = ((p0, 0), (f1, -1), (f2, -2), (f3, -3), (b1, 1), (b2, 2), (b3, 3))
        for ref, off in whole + ((h0, 4),):
            owner = lax.rem(z + off + 8, 8) * 2 + own
            out_copies.append(
                pltpu.make_async_copy(ref.at[pl.ds(0, 48)], wo.at[rows(owner, 48)], sem_o)
            )
            glu_copies.append(
                pltpu.make_async_copy(ref.at[pl.ds(48, 96)], wv.at[rows(owner, 96)], sem_g)
            )
        for ref, off in whole + ((h1, 4),):
            owner = lax.rem(z + off + 8, 8) * 2 + own
            start = 0 if off == 4 else 144
            glu_copies.append(
                pltpu.make_async_copy(ref.at[pl.ds(start, 96)], wg.at[rows(owner, 96)], sem_g)
            )
    for cp in out_copies + glu_copies:
        cp.start()
    for cp in out_copies:
        cp.wait()
    attn = jnp.zeros((ROWS, D), F32)
    for r, ref in enumerate((a0, a1, a2, a3)):
        part = wo[rows(me ^ r, HCOLS), :]
        attn = attn + jnp.dot(ref[:, :HCOLS], part, preferred_element_type=F32)
    resid = (local[...].astype(F32) + attn).astype(BF16)
    resid_ref[...] = resid
    glu_in = norm(resid.astype(F32), gain[...]).astype(BF16)
    for cp in glu_copies:
        cp.wait()
    for j in range(0, D, 512):
        value = jnp.dot(glu_in, wv[:, j : j + 512], preferred_element_type=F32)
        gate = jnp.dot(glu_in, wg[:, j : j + 512], preferred_element_type=F32)
        gated_ref[:, j : j + 512] = (value * jax.nn.sigmoid(gate)).astype(BF16)


def glu(attended, local, gain, rings):
    srcs = []
    for f, b, h0, h1 in rings:
        srcs += [f[0], *f[1:], *b[1:], h0, h1]
    return pl.pallas_call(
        glu_kernel,
        name="glu",
        out_shape=(jax.ShapeDtypeStruct((ROWS, D), BF16),) * 2,
        in_specs=[VM] * 6 + [ANY] * 18,
        out_specs=(VM, VM),
        scratch_shapes=[
            pltpu.VMEM((WIDTH, D), BF16),
            pltpu.VMEM((D, D), BF16),
            pltpu.VMEM((D, D), BF16),
            pltpu.SemaphoreType.DMA,
            pltpu.SemaphoreType.DMA,
        ],
        compiler_params=params(),
        cost_estimate=cost(12),
    )(*attended, local, gain, *srcs)


RB = 32
CT = 4
TILES = D // 128


def conv_kernel(gated, below, above, rim, dw, gain, resid, out, xb, cv):
    for t in range(TILES):
        cols = slice(t * 128, (t + 1) * 128)
        xb[t, :HALF] = below[:, cols].astype(F32)
        xb[t, HALF : HALF + ROWS] = gated[:, cols].astype(F32)
        xb[t, HALF + ROWS :] = above[:, cols].astype(F32)

    @pl.loop(0, TILES // CT)
    def _(group):
        for r0 in range(0, ROWS, RB):
            mine = rim[r0 + HALF : r0 + HALF + RB, :]
            total = [jnp.zeros((RB, 128), F32) for _ in range(CT)]
            for j in range(CONV_K):
                keep = rim[r0 + j : r0 + j + RB, :] == mine
                for t in range(CT):
                    tile = group * CT + t
                    term = xb[tile, r0 + j : r0 + j + RB, :] * dw[tile, j : j + 1, :]
                    total[t] = total[t] + jnp.where(keep, term, 0.0)
            for t in range(CT):
                cv[group * CT + t, r0 : r0 + RB, :] = total[t]

    for r0 in range(0, ROWS, 64):
        parts = [cv[t, r0 : r0 + 64, :] for t in range(TILES)]
        centre = jnp.sum(sum(parts), -1, keepdims=True) * (1.0 / D)
        parts = [p - centre for p in parts]
        spread = jnp.sum(sum(p * p for p in parts), -1, keepdims=True) * (1.0 / D)
        scale = lax.rsqrt(spread + 1e-05)
        for t in range(TILES):
            cols = slice(t * 128, (t + 1) * 128)
            mid = parts[t] * scale * gain[:, cols]
            res = resid[r0 : r0 + 64, cols].astype(F32)
            out[r0 : r0 + 64, cols] = (res + mid * jax.nn.sigmoid(mid)).astype(BF16)


def conv(gated, below, above, rim, dw, gain, resid):
    return pl.pallas_call(
        conv_kernel,
        name="conv",
        out_shape=jax.ShapeDtypeStruct((ROWS, D), BF16),
        in_specs=[VM] * 7,
        out_specs=VM,
        scratch_shapes=[
            pltpu.VMEM((TILES, ROWS + CONV_K, 128), F32),
            pltpu.VMEM((TILES, ROWS, 128), F32),
        ],
        compiler_params=params(),
        cost_estimate=cost(8),
    )(gated, below, above, rim, dw, gain, resid)


def body(
    frames, segment_ids, ln_attn_gain, w_qkv, w_out, ln_conv_gain, w_glu, dw_kernel, ln_mid_gain
):
    local = frames[0]
    xl, y, c = lax.axis_index("xl"), lax.axis_index("y"), lax.axis_index("c")
    group = lax.axis_index("xh") * 2 + c
    first_frame = (y * GROUP + group) * ROWS

    mine = lax.dynamic_index_in_dim(w_qkv.reshape(96, 3, GROUP, HCOLS), group, 2, keepdims=False)
    wq, wk, wv = mine[:, 0], mine[:, 1], mine[:, 2]
    own = jnp.concatenate(
        [wk[:, :128], wv[:, 128:], wk[:, 128:], wv[:, :128], wq[:, :128],
         jnp.zeros((96, HD), BF16), wq[:, 128:]],
        axis=1,
    )
    pair = jnp.concatenate([own, swap(own, "xl", 1, 2)], axis=0)
    qkv_ring = z_ring(pair, 96)

    normed = norm(local.astype(F32), ln_attn_gain).astype(BF16)
    pieces = [normed] + [swap(normed, ("xh", "c"), r, 4) for r in (1, 2, 3)]
    all_segs = lax.all_gather(segment_ids[0], ("y", "xh", "c"), axis=0, tiled=True)

    kv, q = qkv(pieces, qkv_ring)

    both = jnp.concatenate([w_out, w_glu[:, :D], w_glu[:, D:]], axis=0)
    other = lax.ppermute(both, ("xl", "c"), [(1, 2), (2, 1)])
    late = (qkv_ring[2][0, 0] + qkv_ring[3][0, 0]).astype(F32)
    carried = jnp.where(jnp.logical_or(xl == c, late == jnp.inf), both, other)
    f, b, h0, h1 = z_ring(carried, 144)
    over = functools.partial(shift, axis="c", count=2, step=1)
    ring_a = (f, b, h0, h1)
    f0 = over(f[0])
    ring_b = ([f0] + [over(v) for v in f[1:]], [f0] + [over(v) for v in b[1:]], over(h0), over(h1))

    up, down = shift(kv, "y", 4, 1), shift(kv, "y", 4, -1)
    far0 = shift(up[:512], "y", 4, 1)
    far1 = shift(down[512:], "y", 4, -1)

    lo, hi = all_segs[::ROWS], all_segs[ROWS - 1 :: ROWS]
    kseg = all_segs.reshape(LEN // KB, KB)
    my_segs = lax.dynamic_slice_in_dim(all_segs, y * CHUNK, CHUNK)
    qseg = jnp.broadcast_to(my_segs[:, None], (CHUNK, 128))
    common = (q, qseg, kseg, lo, hi)
    state = attend(((0, 0, 1024),), *common, (kv,), None, False, 7)
    state = attend(((-1, 0, 1024), (1, 0, 1024)), *common, (up, down), state, False, 14)
    out = attend(((-2, 0, 512), (2, 512, 512)), *common, (far0, far1), state, True, 7)

    pieces = out.reshape(GROUP, ROWS, 256)
    attended = [lax.dynamic_index_in_dim(pieces, group, 0, keepdims=False)]
    for r in (1, 2, 3):
        sent = lax.dynamic_index_in_dim(pieces, group ^ r, 0, keepdims=False)
        attended.append(swap(sent, ("xh", "c"), r, 4))
    resid, gated = glu(attended, local, ln_conv_gain[None], (ring_a, ring_b))

    seq = ("y", "xh", "c")
    below = lax.ppermute(gated[ROWS - HALF :], seq, [(i, i + 1) for i in range(15)])
    above = lax.ppermute(gated[:HALF], seq, [(i + 1, i) for i in range(15)])
    padded = jnp.pad(all_segs, (HALF, HALF), constant_values=-1)
    rim = lax.dynamic_slice_in_dim(padded, first_frame, ROWS + CONV_K)
    rim = jnp.broadcast_to(rim[:, None], (ROWS + CONV_K, 128))
    dw = jnp.transpose(dw_kernel.reshape(CONV_K, TILES, 128), (1, 0, 2))
    return conv(gated, below, above, rim, dw, ln_mid_gain[None], resid)[None]


def solution(mesh):
    fine = Mesh(mesh.devices.reshape(8, 2, 4, 2, 2), ("z", "xl", "y", "xh", "c"))
    dp, seq = ("z", "xl"), ("y", "xh", "c")
    return jax.shard_map(
        body,
        mesh=fine,
        in_specs=(
            P(dp, seq, None),
            P(dp, seq),
            P(),
            P(dp, None),
            P(dp, None),
            P(),
            P(dp, None),
            P(),
            P(),
        ),
        out_specs=P(dp, seq, None),
        check_vma=False,
    )
```

```python
import functools

import jax
import jax.numpy as jnp
from jax import lax
from jax.experimental import pallas as pl
from jax.experimental.pallas import tpu as pltpu
from jax.sharding import Mesh
from jax.sharding import PartitionSpec as P

D = 1536
HEADS = 12
HD = 64
CONV_K = 32
HALF = CONV_K // 2
IDS = 12
WIDTH = HEADS * HD
ROWS = 256
GROUP = 4
CHUNK = GROUP * ROWS
HCOLS = WIDTH // GROUP
LEN = 4096
KB = 512
QT = 512
NEG = -1e30
F32, BF16 = jnp.float32, jnp.bfloat16
ANY = pl.BlockSpec(memory_space=pl.ANY)
VM = pl.BlockSpec(memory_space=pltpu.VMEM)
SM = pl.BlockSpec(memory_space=pltpu.SMEM)


def params(limit_mib):
    return pltpu.CompilerParams(vmem_limit_bytes=limit_mib << 20)


def cost(us):
    return pl.CostEstimate(flops=int(us * 9e8), bytes_accessed=int(us * 2e6), transcendentals=0)


def shift(value, axis, count, step):
    return lax.ppermute(value, axis, [(i, (i + step) % count) for i in range(count)])


def swap(value, axes, mask, count):
    return lax.ppermute(value, axes, [(i, i ^ mask) for i in range(count)])


def along_z(value):
    pairs = []
    for i in range(8):
        pairs += [(2 * i, (i + 1) % 8 * 2), (2 * i + 1, (i + 7) % 8 * 2 + 1)]
    return lax.ppermute(value, ("z", "c"), pairs)


def along_x(value):
    def index(x, c):
        return x % 2 * 4 + x // 2 * 2 + c

    pairs = []
    for x in range(4):
        pairs += [(index(x, 0), index((x + 1) % 4, 0)), (index(x, 1), index((x + 3) % 4, 1))]
    return lax.ppermute(value, ("xl", "xh", "c"), pairs)


def between_cores(value):
    return lax.ppermute(value, "c", [(0, 1), (1, 0)])


def norm(values, gain):
    centre = jnp.mean(values, -1, keepdims=True)
    shifted = values - centre
    spread = jnp.mean(shifted * shifted, -1, keepdims=True)
    return shifted * lax.rsqrt(spread + 1e-05) * gain


def z_owner(z, c, k, own):
    sign = (2 * c - 1) if own else (1 - 2 * c)
    return lax.rem(z + sign * k + 8, 8)


def qkv_kernel(n0, n1, n2, n3, *refs):
    srcs, (kv_ref, q_ref, w, sem) = refs[:8], refs[8:]
    z, xl, c = lax.axis_index("z"), lax.axis_index("xl"), lax.axis_index("c")
    me = lax.axis_index("xh") * 2 + c
    cols = pl.ds(pl.multiple_of(c * 640, 640), 640)
    copies = []
    for i, ref in enumerate(srcs):
        zz = z_owner(z, c, i, True) if i < 5 else z_owner(z, c, i - 4, False)
        for half in range(2):
            owner = zz * 2 + (xl if half == 0 else 1 - xl)
            rows = pl.ds(pl.multiple_of(owner * 96, 96), 96)
            copies.append(
                pltpu.make_async_copy(ref.at[pl.ds(half * 96, 96), cols], w.at[rows], sem)
            )
    for cp in copies:
        cp.start()
    for cp in copies:
        cp.wait()
    for r, ref in enumerate((n0, n1, n2, n3)):
        rows = pl.ds(pl.multiple_of((me ^ r) * ROWS, ROWS), ROWS)
        out = jnp.dot(ref[...], w[...], preferred_element_type=F32).astype(BF16)
        kv_ref[rows, :] = out[:, :384]
        q_ref[rows, :] = out[:, 384:]


def qkv(normed, srcs):
    return pl.pallas_call(
        qkv_kernel,
        name="qkv",
        out_shape=(
            jax.ShapeDtypeStruct((CHUNK, 384), BF16),
            jax.ShapeDtypeStruct((CHUNK, 256), BF16),
        ),
        in_specs=[VM] * 4 + [ANY] * 8,
        out_specs=(VM, VM),
        scratch_shapes=[pltpu.VMEM((D, 640), BF16), pltpu.SemaphoreType.DMA],
        compiler_params=params(12),
        cost_estimate=cost(5),
    )(*normed, *srcs)


def attn_kernel(parts, first, last, scal, q_ref, span, *refs):
    kvs, refs = refs[: len(parts)], refs[len(parts) :]
    if first:
        outs, (qs, vt, m, l, acc) = refs[:-5], refs[-5:]
    else:
        (ml_in, acc_in), outs, (qs, vt, m, l, acc) = refs[:2], refs[2:-5], refs[-5:]
    y = lax.axis_index("y")
    tile = pl.program_id(0)
    offs = [sum(p[2] for p in parts[:i]) // KB for i in range(len(parts))]

    @pl.when(tile == 0)
    def _():
        for kv, off, (_, _, count) in zip(kvs, offs, parts):
            for i in range(count // KB):
                rows = slice(i * KB, (i + 1) * KB)
                vt[off + i, :128] = kv[rows, 256:].T
                vt[off + i, 128:] = kv[rows, 128:256].T[:HD]

    low = lax.broadcasted_iota(jnp.int32, (QT, 128), 1) < HD
    qa, qb = q_ref[:, :128] * BF16(0.125), q_ref[:, 128:] * BF16(0.125)
    zero = jnp.zeros_like(qa)
    qs[0] = jnp.where(low, qa, zero)
    qs[1] = jnp.where(low, zero, qa)
    qs[2] = qb
    if first:
        m[...] = jnp.full_like(m, NEG)
        l[...] = jnp.zeros_like(l)
        acc[...] = jnp.zeros_like(acc)
    else:
        m[...] = ml_in[:8]
        l[...] = ml_in[8:]
        acc[...] = acc_in[...]
    s_first, e_first, s_last, e_last = [scal[tile * 4 + i] for i in range(4)]

    def step(kv, row, block, base, masked):
        if masked:
            frame = lax.broadcasted_iota(jnp.int32, (KB, QT), 0) + base
            keep = jnp.logical_and(frame >= span[0:1, :], frame < span[1:2, :])
        scores = [
            lax.dot_general(
                kv[pl.ds(row, KB), :128] if h < 2 else kv[pl.ds(row, KB), 128:256],
                qs[h],
                (((1,), (1,)), ((), ())),
                preferred_element_type=F32,
            )
            for h in range(3)
        ]
        for h in range(3):
            s = jnp.where(keep, scores[h], NEG) if masked else scores[h]
            old = m[h : h + 1]
            new = jnp.maximum(old, jnp.max(s, axis=0, keepdims=True))
            p = jnp.exp(s - new)
            alpha = jnp.exp(old - new)
            m[h : h + 1] = new
            l[h : h + 1] = alpha * l[h : h + 1] + jnp.sum(p, axis=0, keepdims=True)
            rows = slice(h * HD, (h + 1) * HD)
            pv = jnp.dot(vt[block, rows], p.astype(BF16), preferred_element_type=F32)
            acc[rows] = alpha * acc[rows] + pv

    for kv, block, (off, start, count) in zip(kvs, offs, parts):
        begin = lax.rem(y + off + 4, 4) * CHUNK + start
        low_i = jnp.clip(lax.div(jnp.maximum(s_first - begin, 0), KB), 0, count // KB)
        high_i = jnp.clip(lax.div(jnp.maximum(e_last - begin, 0) + KB - 1, KB), 0, count // KB)

        @pl.loop(low_i, high_i)
        def _(i):
            base = begin + i * KB
            row = pl.multiple_of(i * KB, KB)
            plain = jnp.logical_and(s_last <= base, e_first >= base + KB)

            @pl.when(plain)
            def _():
                step(kv, row, block + i, base, False)

            @pl.when(jnp.logical_not(plain))
            def _():
                step(kv, row, block + i, base, True)

    if last:
        (out,) = outs
        for h in range(3):
            rows = slice(h * HD, (h + 1) * HD)
            acc[rows] = acc[rows] / l[h : h + 1]
        out[:, :128] = acc[:128].T.astype(BF16)
        tail = jnp.concatenate([acc[128:], jnp.zeros((HD, QT), F32)], 0)
        out[:, 128:] = tail.T.astype(BF16)
    else:
        ml_out, acc_out = outs
        ml_out[:8] = m[...]
        ml_out[8:] = l[...]
        acc_out[...] = acc[...]


def attend(parts, q, span, scal, kvs, state, last, us):
    first = state is None

    def rows(count):
        return pl.BlockSpec((QT, count), lambda i: (i, 0))

    def cols(count):
        return pl.BlockSpec((count, QT), lambda i: (0, i))

    state_shapes = (
        jax.ShapeDtypeStruct((16, CHUNK), F32),
        jax.ShapeDtypeStruct((HCOLS, CHUNK), F32),
    )
    return pl.pallas_call(
        functools.partial(attn_kernel, parts, first, last),
        name="attend",
        grid=(CHUNK // QT,),
        out_shape=jax.ShapeDtypeStruct((CHUNK, 256), BF16) if last else state_shapes,
        in_specs=[SM, rows(256), cols(8)]
        + [VM] * len(kvs)
        + ([] if first else [cols(16), cols(HCOLS)]),
        out_specs=rows(256) if last else (cols(16), cols(HCOLS)),
        scratch_shapes=[
            pltpu.VMEM((3, QT, 128), BF16),
            pltpu.VMEM((sum(p[2] for p in parts) // KB, HCOLS, KB), BF16),
            pltpu.VMEM((8, QT), F32),
            pltpu.VMEM((8, QT), F32),
            pltpu.VMEM((HCOLS, QT), F32),
        ],
        compiler_params=params(18),
        cost_estimate=cost(us),
    )(scal, q, span, *kvs, *(() if first else state))


def glu_kernel(a0, a1, a2, a3, local, gain, *refs):
    srcs, (resid_ref, gated_ref, wo, wv, wg, sem_o, sem_g) = refs[:16], refs[16:]
    z, xl, c = lax.axis_index("z"), lax.axis_index("xl"), lax.axis_index("c")
    me = lax.axis_index("xh") * 2 + c
    out_copies, glu_copies = [], []

    def rows(owner, count):
        return pl.ds(pl.multiple_of(owner * count, count), count)

    for half in range(2):
        for i in range(8):
            ref = srcs[8 * half + i]
            zz = z_owner(z, c, i, True) if i < 5 else z_owner(z, c, i - 4, False)
            owner = zz * 2 + (xl if half == 0 else 1 - xl)
            out_copies.append(
                pltpu.make_async_copy(ref.at[pl.ds(0, 48)], wo.at[rows(owner, 48)], sem_o)
            )
            glu_copies.append(
                pltpu.make_async_copy(ref.at[pl.ds(48, 96)], wv.at[rows(owner, 96)], sem_g)
            )
            glu_copies.append(
                pltpu.make_async_copy(ref.at[pl.ds(144, 96)], wg.at[rows(owner, 96)], sem_g)
            )
    for cp in out_copies + glu_copies:
        cp.start()
    for cp in out_copies:
        cp.wait()
    attn = jnp.zeros((ROWS, D), F32)
    for r, ref in enumerate((a0, a1, a2, a3)):
        part = wo[rows(me ^ r, HCOLS), :]
        attn = attn + jnp.dot(ref[:, :HCOLS], part, preferred_element_type=F32)
    resid = (local[...].astype(F32) + attn).astype(BF16)
    resid_ref[...] = resid
    glu_in = norm(resid.astype(F32), gain[...]).astype(BF16)
    for cp in glu_copies:
        cp.wait()
    for j in range(0, D, 512):
        value = jnp.dot(glu_in, wv[:, j : j + 512], preferred_element_type=F32)
        gate = jnp.dot(glu_in, wg[:, j : j + 512], preferred_element_type=F32)
        gated_ref[:, j : j + 512] = (value * jax.nn.sigmoid(gate)).astype(BF16)


def glu(attended, local, gain, srcs):
    return pl.pallas_call(
        glu_kernel,
        name="glu",
        out_shape=(jax.ShapeDtypeStruct((ROWS, D), BF16),) * 2,
        in_specs=[VM] * 6 + [ANY] * 16,
        out_specs=(VM, VM),
        scratch_shapes=[
            pltpu.VMEM((WIDTH, D), BF16),
            pltpu.VMEM((D, D), BF16),
            pltpu.VMEM((D, D), BF16),
            pltpu.SemaphoreType.DMA,
            pltpu.SemaphoreType.DMA,
        ],
        compiler_params=params(26),
        cost_estimate=cost(10),
    )(*attended, local, gain, *srcs)


RB = 32
CT = 4
TILES = D // 128


def conv_kernel(scal, gated, below, above, taps, dw, gain, resid, out, xb, cv):
    for t in range(TILES):
        cols = slice(t * 128, (t + 1) * 128)
        xb[t, :HALF] = below[:, cols].astype(F32)
        xb[t, HALF : HALF + ROWS] = gated[:, cols].astype(F32)
        xb[t, HALF + ROWS :] = above[:, cols].astype(F32)

    def block(r0, group, masked):
        total = [jnp.zeros((RB, 128), F32) for _ in range(CT)]
        if masked:
            begin, end = taps[0, pl.ds(r0, RB), :], taps[1, pl.ds(r0, RB), :]
        for j in range(CONV_K):
            if masked:
                keep = jnp.logical_and(begin <= j, j < end)
            for t in range(CT):
                tile = group * CT + t
                term = xb[tile, pl.ds(r0 + j, RB), :] * dw[tile, j : j + 1, :]
                total[t] = total[t] + (jnp.where(keep, term, 0.0) if masked else term)
        for t in range(CT):
            cv[group * CT + t, pl.ds(r0, RB), :] = total[t]

    @pl.loop(0, ROWS // RB)
    def _(i):
        r0 = pl.multiple_of(i * RB, RB)

        @pl.loop(0, TILES // CT)
        def _(group):
            @pl.when(scal[i] == 1)
            def _():
                block(r0, group, False)

            @pl.when(scal[i] == 0)
            def _():
                block(r0, group, True)

    @pl.loop(0, ROWS // 64)
    def _(i):
        rows = pl.ds(pl.multiple_of(i * 64, 64), 64)
        parts = [cv[t, rows, :] for t in range(TILES)]
        centre = jnp.sum(sum(parts), -1, keepdims=True) * (1.0 / D)
        parts = [p - centre for p in parts]
        spread = jnp.sum(sum(p * p for p in parts), -1, keepdims=True) * (1.0 / D)
        scale = lax.rsqrt(spread + 1e-05)
        for t in range(TILES):
            cols = slice(t * 128, (t + 1) * 128)
            mid = parts[t] * scale * gain[:, cols]
            res = resid[rows, cols].astype(F32)
            out[rows, cols] = (res + mid * jax.nn.sigmoid(mid)).astype(BF16)


def conv(scal, gated, below, above, taps, dw, gain, resid):
    return pl.pallas_call(
        conv_kernel,
        name="conv",
        out_shape=jax.ShapeDtypeStruct((ROWS, D), BF16),
        in_specs=[SM] + [VM] * 7,
        out_specs=VM,
        scratch_shapes=[
            pltpu.VMEM((TILES, ROWS + CONV_K, 128), F32),
            pltpu.VMEM((TILES, ROWS, 128), F32),
        ],
        compiler_params=params(14),
        cost_estimate=cost(8),
    )(scal, gated, below, above, taps, dw, gain, resid)


def body(
    frames, segment_ids, ln_attn_gain, w_qkv, w_out, ln_conv_gain, w_glu, dw_kernel, ln_mid_gain
):
    local = frames[0]
    y, xh, c = lax.axis_index("y"), lax.axis_index("xh"), lax.axis_index("c")
    group = xh * 2 + c
    first_frame = (y * GROUP + group) * ROWS

    wq, wk, wv = [
        lax.dynamic_slice_in_dim(w_qkv, part * WIDTH + xh * 2 * HCOLS, 2 * HCOLS, 1)
        for part in range(3)
    ]
    columns = []
    for j in (0, HCOLS):
        columns += [wk[:, j : j + 128], wv[:, j + 128 : j + HCOLS], wk[:, j + 128 : j + HCOLS]]
        columns += [wv[:, j : j + 128], wq[:, j : j + 128], jnp.zeros((96, HD), BF16)]
        columns += [wq[:, j + 128 : j + HCOLS]]
    own = jnp.concatenate(columns, axis=1)
    ring = [jnp.concatenate([own, swap(own, "xl", 1, 2)], axis=0)]
    for _ in range(4):
        ring.append(along_z(ring[-1]))
    srcs = ring + [between_cores(v) for v in ring[1:4]]

    normed = norm(local.astype(F32), ln_attn_gain).astype(BF16)
    n2 = swap(normed, "xh", 1, 2)
    pieces = [normed, between_cores(normed), n2, between_cores(n2)]
    kv, q = qkv(pieces, srcs)

    both = jnp.concatenate([w_out, w_glu[:, :D], w_glu[:, D:]], axis=0)
    late = (ring[4][0, 0] + n2[0, 0]).astype(F32)
    z_set = [jnp.where(late == jnp.inf, jnp.zeros_like(both), both)]
    for _ in range(4):
        z_set.append(along_z(z_set[-1]))
    x_set = [along_x(v) for v in z_set]
    weights = []
    for values in (z_set, x_set):
        weights += values + [between_cores(v) for v in values[1:4]]

    ids = lax.broadcasted_iota(jnp.int32, (IDS, ROWS), 0)
    counts = jnp.sum((segment_ids == ids).astype(jnp.int32), axis=1)[None]
    for axis, mask, count in (("c", 1, 2), ("xh", 1, 2), ("y", 1, 4), ("y", 2, 4)):
        counts = counts + swap(counts, axis, mask, count)
    ends = jnp.cumsum(counts[0])
    starts = ends - counts[0]

    def spans(frame):
        begin = jnp.max(jnp.where(starts[:, None] <= frame[None], starts[:, None], 0), 0)
        end = jnp.min(jnp.where(ends[:, None] > frame[None], ends[:, None], LEN), 0)
        return begin, end

    begin, end = spans(y * CHUNK + jnp.arange(CHUNK, dtype=jnp.int32))
    span = jnp.concatenate([begin[None], end[None], jnp.zeros((6, CHUNK), jnp.int32)], 0)
    firsts, lasts = slice(0, None, QT), slice(QT - 1, None, QT)
    scal = jnp.stack([begin[firsts], end[firsts], begin[lasts], end[lasts]], 1).reshape(-1)

    up, down = shift(kv, "y", 4, 1), shift(kv, "y", 4, -1)
    far0 = shift(up[:512], "y", 4, 1)
    far1 = shift(down[512:], "y", 4, -1)
    common = (q, span, scal)
    state = attend(((0, 0, 1024),), *common, (kv,), None, False, 7)
    state = attend(((-1, 0, 1024), (1, 0, 1024)), *common, (up, down), state, False, 14)
    out = attend(((-2, 0, 512), (2, 512, 512)), *common, (far0, far1), state, True, 7)

    pieces = out.reshape(GROUP, ROWS, 256)
    attended = [lax.dynamic_index_in_dim(pieces, group, 0, keepdims=False)]
    for r in (1, 2, 3):
        sent = lax.dynamic_index_in_dim(pieces, group ^ r, 0, keepdims=False)
        attended.append(swap(sent, ("xh", "c"), r, 4))
    resid, gated = glu(attended, local, ln_conv_gain[None], weights)

    seq = ("y", "xh", "c")
    below = lax.ppermute(gated[ROWS - HALF :], seq, [(i, i + 1) for i in range(15)])
    above = lax.ppermute(gated[:HALF], seq, [(i + 1, i) for i in range(15)])
    frame = first_frame + jnp.arange(ROWS, dtype=jnp.int32)
    begin, end = spans(frame)
    taps = jnp.stack([begin - frame + HALF, end - frame + HALF], 0)
    blocks = slice(0, None, RB), slice(RB - 1, None, RB)
    plain = jnp.logical_and(
        begin[blocks[1]] <= frame[blocks[0]] - HALF, end[blocks[0]] >= frame[blocks[1]] + HALF
    ).astype(jnp.int32)
    taps = jnp.broadcast_to(taps[:, :, None], (2, ROWS, 128))
    dw = jnp.transpose(dw_kernel.reshape(CONV_K, TILES, 128), (1, 0, 2))
    return conv(plain, gated, below, above, taps, dw, ln_mid_gain[None], resid)[None]


def solution(mesh):
    fine = Mesh(mesh.devices.reshape(8, 2, 4, 2, 2), ("z", "xl", "y", "xh", "c"))
    dp, seq = ("z", "xl"), ("y", "xh", "c")
    return jax.shard_map(
        body,
        mesh=fine,
        in_specs=(
            P(dp, seq, None),
            P(dp, seq),
            P(),
            P(dp, None),
            P(dp, None),
            P(),
            P(dp, None),
            P(),
            P(),
        ),
        out_specs=P(dp, seq, None),
        check_vma=False,
    )
```

```python
import functools

import jax
import jax.numpy as jnp
from jax import lax
from jax.experimental import pallas as pl
from jax.experimental.pallas import tpu as pltpu
from jax.sharding import Mesh
from jax.sharding import PartitionSpec as P

D = 1536
HEADS = 12
HD = 64
CONV_K = 32
HALF = CONV_K // 2
IDS = 12
WIDTH = HEADS * HD
ROWS = 256
GROUP = 4
CHUNK = GROUP * ROWS
HCOLS = WIDTH // GROUP
LEN = 4096
KB = 512
QT = 512
NEG = -1e30
F32, BF16 = jnp.float32, jnp.bfloat16
ANY = pl.BlockSpec(memory_space=pl.ANY)
VM = pl.BlockSpec(memory_space=pltpu.VMEM)
SM = pl.BlockSpec(memory_space=pltpu.SMEM)


def params(limit_mib):
    return pltpu.CompilerParams(vmem_limit_bytes=limit_mib << 20)


def cost(us):
    return pl.CostEstimate(flops=int(us * 9e8), bytes_accessed=int(us * 2e6), transcendentals=0)


def shift(value, axis, count, step):
    return lax.ppermute(value, axis, [(i, (i + step) % count) for i in range(count)])


def swap(value, axes, mask, count):
    return lax.ppermute(value, axes, [(i, i ^ mask) for i in range(count)])


def along_z(value):
    pairs = []
    for i in range(8):
        pairs += [(2 * i, (i + 1) % 8 * 2), (2 * i + 1, (i + 7) % 8 * 2 + 1)]
    return lax.ppermute(value, ("z", "c"), pairs)


def along_x(value):
    def index(x, c):
        return x % 2 * 4 + x // 2 * 2 + c

    pairs = []
    for x in range(4):
        pairs += [(index(x, 0), index((x + 1) % 4, 0)), (index(x, 1), index((x + 3) % 4, 1))]
    return lax.ppermute(value, ("xl", "xh", "c"), pairs)


def tie(*values):
    return lax.optimization_barrier(values)


def between_cores(value):
    return lax.ppermute(value, "c", [(0, 1), (1, 0)])


def norm(values, gain):
    centre = jnp.mean(values, -1, keepdims=True)
    shifted = values - centre
    spread = jnp.mean(shifted * shifted, -1, keepdims=True)
    return shifted * lax.rsqrt(spread + 1e-05) * gain


def z_owner(z, c, k, own):
    sign = (2 * c - 1) if own else (1 - 2 * c)
    return lax.rem(z + sign * k + 8, 8)


def qkv_kernel(n0, n1, n2, n3, *refs):
    srcs, (kv_ref, q_ref, w, sem) = refs[:8], refs[8:]
    z, xl, c = lax.axis_index("z"), lax.axis_index("xl"), lax.axis_index("c")
    me = lax.axis_index("xh") * 2 + c
    cols = pl.ds(pl.multiple_of(c * 640, 640), 640)
    copies = []
    for i, ref in enumerate(srcs):
        zz = z_owner(z, c, i, True) if i < 5 else z_owner(z, c, i - 4, False)
        for half in range(2):
            owner = zz * 2 + (xl if half == 0 else 1 - xl)
            rows = pl.ds(pl.multiple_of(owner * 96, 96), 96)
            copies.append(
                pltpu.make_async_copy(ref.at[pl.ds(half * 96, 96), cols], w.at[rows], sem)
            )
    for cp in copies:
        cp.start()
    for cp in copies:
        cp.wait()
    for r, ref in enumerate((n0, n1, n2, n3)):
        rows = pl.ds(pl.multiple_of((me ^ r) * ROWS, ROWS), ROWS)
        out = jnp.dot(ref[...], w[...], preferred_element_type=F32).astype(BF16)
        kv_ref[rows, :] = out[:, :384]
        q_ref[rows, :] = out[:, 384:]


def qkv(normed, srcs):
    return pl.pallas_call(
        qkv_kernel,
        name="qkv",
        out_shape=(
            jax.ShapeDtypeStruct((CHUNK, 384), BF16),
            jax.ShapeDtypeStruct((CHUNK, 256), BF16),
        ),
        in_specs=[VM] * 4 + [ANY] * 8,
        out_specs=(VM, VM),
        scratch_shapes=[pltpu.VMEM((D, 640), BF16), pltpu.SemaphoreType.DMA],
        compiler_params=params(12),
        cost_estimate=cost(5),
    )(*normed, *srcs)


def attn_kernel(parts, first, last, scal, q_ref, span, *refs):
    kvs, refs = refs[: len(parts)], refs[len(parts) :]
    if first:
        outs, (qs, keys, vt, m, l, acc) = refs[:-6], refs[-6:]
    else:
        (ml_in, acc_in), outs, (qs, keys, vt, m, l, acc) = refs[:2], refs[2:-6], refs[-6:]
    y = lax.axis_index("y")
    tile = pl.program_id(0)

    @pl.when(tile == 0)
    def _():
        for kv, (_, start, count) in zip(kvs, parts):
            for i in range(count // KB):
                rows, block = slice(i * KB, (i + 1) * KB), start // KB + i
                for half in range(2):
                    keys[half, block * KB : (block + 1) * KB] = kv[
                        rows, half * 128 : (half + 1) * 128
                    ]
                vt[block, :128] = kv[rows, 256:].T
                vt[block, 128:] = kv[rows, 128:256].T[:HD]

    low = lax.broadcasted_iota(jnp.int32, (QT, 128), 1) < HD
    qa, qb = q_ref[:, :128] * BF16(0.125), q_ref[:, 128:] * BF16(0.125)
    zero = jnp.zeros_like(qa)
    qs[0] = jnp.where(low, qa, zero)
    qs[1] = jnp.where(low, zero, qa)
    qs[2] = qb
    if first:
        m[...] = jnp.full_like(m, NEG)
        l[...] = jnp.zeros_like(l)
        acc[...] = jnp.zeros_like(acc)
    else:
        m[...] = ml_in[:8]
        l[...] = ml_in[8:]
        acc[...] = acc_in[...]
    s_first, e_first, s_last, e_last = [scal[tile * 4 + i] for i in range(4)]

    def score(h, half, row):
        return lax.dot_general(
            keys[half, pl.ds(row, KB), :],
            qs[h],
            (((1,), (1,)), ((), ())),
            preferred_element_type=F32,
        )

    def update(h, s, block):
        old = m[pl.ds(h, 1)]
        new = jnp.maximum(old, jnp.max(s, axis=0, keepdims=True))
        p = jnp.exp(s - new)
        alpha = jnp.exp(old - new)
        m[pl.ds(h, 1)] = new
        l[pl.ds(h, 1)] = alpha * l[pl.ds(h, 1)] + jnp.sum(p, axis=0, keepdims=True)
        rows = pl.ds(h * HD if isinstance(h, int) else pl.multiple_of(h * HD, HD), HD)
        pv = jnp.dot(vt[block, rows], p.astype(BF16), preferred_element_type=F32)
        acc[rows] = alpha * acc[rows] + pv

    begin = lax.rem(y + parts[0][0] + 4, 4) * CHUNK
    low_i = jnp.clip(lax.div(jnp.maximum(s_first - begin, 0), KB), 0, CHUNK // KB)
    high_i = jnp.clip(lax.div(jnp.maximum(e_last - begin, 0) + KB - 1, KB), 0, CHUNK // KB)

    @pl.loop(low_i, high_i)
    def _(i):
        base = begin + i * KB
        row = pl.multiple_of(i * KB, KB)
        plain = jnp.logical_and(s_last <= base, e_first >= base + KB)

        @pl.when(plain)
        def _():
            scores = [score(h, h // 2, row) for h in range(3)]
            for h in range(3):
                update(h, scores[h], i)

        @pl.when(jnp.logical_not(plain))
        def _():
            @pl.loop(0, 3)
            def _(h):
                frame = lax.broadcasted_iota(jnp.int32, (KB, QT), 0) + base
                keep = jnp.logical_and(frame >= span[0:1, :], frame < span[1:2, :])
                update(h, jnp.where(keep, score(h, lax.div(h, 2), row), NEG), i)

    if last:
        (out,) = outs
        for h in range(3):
            rows = slice(h * HD, (h + 1) * HD)
            acc[rows] = acc[rows] / l[h : h + 1]
        out[:, :128] = acc[:128].T.astype(BF16)
        tail = jnp.concatenate([acc[128:], jnp.zeros((HD, QT), F32)], 0)
        out[:, 128:] = tail.T.astype(BF16)
    else:
        ml_out, acc_out = outs
        ml_out[:8] = m[...]
        ml_out[8:] = l[...]
        acc_out[...] = acc[...]


def attend(parts, q, span, scal, kvs, state, last, us):
    first = state is None

    def rows(count):
        return pl.BlockSpec((QT, count), lambda i: (i, 0))

    def cols(count):
        return pl.BlockSpec((count, QT), lambda i: (0, i))

    state_shapes = (
        jax.ShapeDtypeStruct((16, CHUNK), F32),
        jax.ShapeDtypeStruct((HCOLS, CHUNK), F32),
    )
    return pl.pallas_call(
        functools.partial(attn_kernel, parts, first, last),
        name="attend",
        grid=(CHUNK // QT,),
        out_shape=jax.ShapeDtypeStruct((CHUNK, 256), BF16) if last else state_shapes,
        in_specs=[SM, rows(256), cols(8)]
        + [VM] * len(kvs)
        + ([] if first else [cols(16), cols(HCOLS)]),
        out_specs=rows(256) if last else (cols(16), cols(HCOLS)),
        scratch_shapes=[
            pltpu.VMEM((3, QT, 128), BF16),
            pltpu.VMEM((2, CHUNK, 128), BF16),
            pltpu.VMEM((CHUNK // KB, HCOLS, KB), BF16),
            pltpu.VMEM((8, QT), F32),
            pltpu.VMEM((8, QT), F32),
            pltpu.VMEM((HCOLS, QT), F32),
        ],
        compiler_params=params(18),
        cost_estimate=cost(us),
    )(scal, q, span, *kvs, *(() if first else state))


def glu_kernel(a0, a1, a2, a3, local, gain, *refs):
    srcs, (resid_ref, gated_ref, wo, wv, wg, sem_o, sem_g) = refs[:16], refs[16:]
    z, xl, c = lax.axis_index("z"), lax.axis_index("xl"), lax.axis_index("c")
    me = lax.axis_index("xh") * 2 + c
    out_copies, glu_copies = [], []

    def rows(owner, count):
        return pl.ds(pl.multiple_of(owner * count, count), count)

    for half in range(2):
        for i in range(8):
            ref = srcs[8 * half + i]
            zz = z_owner(z, c, i, True) if i < 5 else z_owner(z, c, i - 4, False)
            owner = zz * 2 + (xl if half == 0 else 1 - xl)
            out_copies.append(
                pltpu.make_async_copy(ref.at[pl.ds(0, 48)], wo.at[rows(owner, 48)], sem_o)
            )
            glu_copies.append(
                pltpu.make_async_copy(ref.at[pl.ds(48, 96)], wv.at[rows(owner, 96)], sem_g)
            )
            glu_copies.append(
                pltpu.make_async_copy(ref.at[pl.ds(144, 96)], wg.at[rows(owner, 96)], sem_g)
            )
    for cp in out_copies + glu_copies:
        cp.start()
    for cp in out_copies:
        cp.wait()
    attn = jnp.zeros((ROWS, D), F32)
    for r, ref in enumerate((a0, a1, a2, a3)):
        part = wo[rows(me ^ r, HCOLS), :]
        attn = attn + jnp.dot(ref[:, :HCOLS], part, preferred_element_type=F32)
    resid = (local[...].astype(F32) + attn).astype(BF16)
    resid_ref[...] = resid
    glu_in = norm(resid.astype(F32), gain[...]).astype(BF16)
    for cp in glu_copies:
        cp.wait()
    for j in range(0, D, 512):
        value = jnp.dot(glu_in, wv[:, j : j + 512], preferred_element_type=F32)
        gate = jnp.dot(glu_in, wg[:, j : j + 512], preferred_element_type=F32)
        gated_ref[:, j : j + 512] = (value * jax.nn.sigmoid(gate)).astype(BF16)


def glu(attended, local, gain, srcs):
    return pl.pallas_call(
        glu_kernel,
        name="glu",
        out_shape=(jax.ShapeDtypeStruct((ROWS, D), BF16),) * 2,
        in_specs=[VM] * 6 + [ANY] * 16,
        out_specs=(VM, VM),
        scratch_shapes=[
            pltpu.VMEM((WIDTH, D), BF16),
            pltpu.VMEM((D, D), BF16),
            pltpu.VMEM((D, D), BF16),
            pltpu.SemaphoreType.DMA,
            pltpu.SemaphoreType.DMA,
        ],
        compiler_params=params(26),
        cost_estimate=cost(10),
    )(*attended, local, gain, *srcs)


RB = 32
CT = 4
TILES = D // 128


def conv_kernel(scal, gated, below, above, taps, dw, gain, resid, out, xb, cv):
    for t in range(TILES):
        cols = slice(t * 128, (t + 1) * 128)
        xb[t, :HALF] = below[:, cols].astype(F32)
        xb[t, HALF : HALF + ROWS] = gated[:, cols].astype(F32)
        xb[t, HALF + ROWS :] = above[:, cols].astype(F32)

    def block(r0, group, masked):
        total = [jnp.zeros((RB, 128), F32) for _ in range(CT)]
        if masked:
            begin, end = taps[0, pl.ds(r0, RB), :], taps[1, pl.ds(r0, RB), :]
        for j in range(CONV_K):
            if masked:
                keep = jnp.logical_and(begin <= j, j < end)
            for t in range(CT):
                tile = group * CT + t
                term = xb[tile, pl.ds(r0 + j, RB), :] * dw[tile, j : j + 1, :]
                total[t] = total[t] + (jnp.where(keep, term, 0.0) if masked else term)
        for t in range(CT):
            cv[group * CT + t, pl.ds(r0, RB), :] = total[t]

    @pl.loop(0, ROWS // RB)
    def _(i):
        r0 = pl.multiple_of(i * RB, RB)

        @pl.loop(0, TILES // CT)
        def _(group):
            @pl.when(scal[i] == 1)
            def _():
                block(r0, group, False)

            @pl.when(scal[i] == 0)
            def _():
                block(r0, group, True)

    @pl.loop(0, ROWS // 64)
    def _(i):
        rows = pl.ds(pl.multiple_of(i * 64, 64), 64)
        parts = [cv[t, rows, :] for t in range(TILES)]
        centre = jnp.sum(sum(parts), -1, keepdims=True) * (1.0 / D)
        parts = [p - centre for p in parts]
        spread = jnp.sum(sum(p * p for p in parts), -1, keepdims=True) * (1.0 / D)
        scale = lax.rsqrt(spread + 1e-05)
        for t in range(TILES):
            cols = slice(t * 128, (t + 1) * 128)
            mid = parts[t] * scale * gain[:, cols]
            res = resid[rows, cols].astype(F32)
            out[rows, cols] = (res + mid * jax.nn.sigmoid(mid)).astype(BF16)


def conv(scal, gated, below, above, taps, dw, gain, resid):
    return pl.pallas_call(
        conv_kernel,
        name="conv",
        out_shape=jax.ShapeDtypeStruct((ROWS, D), BF16),
        in_specs=[SM] + [VM] * 7,
        out_specs=VM,
        scratch_shapes=[
            pltpu.VMEM((TILES, ROWS + CONV_K, 128), F32),
            pltpu.VMEM((TILES, ROWS, 128), F32),
        ],
        compiler_params=params(14),
        cost_estimate=cost(8),
    )(scal, gated, below, above, taps, dw, gain, resid)


def body(
    frames, segment_ids, ln_attn_gain, w_qkv, w_out, ln_conv_gain, w_glu, dw_kernel, ln_mid_gain
):
    local = frames[0]
    y, xh, c = lax.axis_index("y"), lax.axis_index("xh"), lax.axis_index("c")
    group = xh * 2 + c
    first_frame = (y * GROUP + group) * ROWS

    wq, wk, wv = [
        lax.dynamic_slice_in_dim(w_qkv, part * WIDTH + xh * 2 * HCOLS, 2 * HCOLS, 1)
        for part in range(3)
    ]
    columns = []
    for j in (0, HCOLS):
        columns += [wk[:, j : j + 128], wv[:, j + 128 : j + HCOLS], wk[:, j + 128 : j + HCOLS]]
        columns += [wv[:, j : j + 128], wq[:, j : j + 128], jnp.zeros((96, HD), BF16)]
        columns += [wq[:, j + 128 : j + HCOLS]]
    own = jnp.concatenate(columns, axis=1)
    ids = lax.broadcasted_iota(jnp.int32, (IDS, ROWS), 0)
    counts = jnp.sum((segment_ids == ids).astype(jnp.int32), axis=1)[None]
    hops = (("c", 1, 2), ("xh", 1, 2), ("y", 1, 4), ("y", 2, 4))
    ring = [jnp.concatenate([own, swap(own, "xl", 1, 2)], axis=0)]
    for axis, mask, count in hops:
        counts = counts + swap(counts, axis, mask, count)
        src, counts = tie(ring[-1], counts)
        ring.append(along_z(src))
    srcs = ring + [between_cores(v) for v in ring[1:4]]

    normed = norm(local.astype(F32), ln_attn_gain).astype(BF16)
    n2, srcs[3] = tie(swap(normed, "xh", 1, 2), ring[3])
    pieces = [normed, between_cores(normed), n2, between_cores(n2)]
    kv, q = qkv(pieces, srcs)

    ends = jnp.cumsum(counts[0])
    starts = ends - counts[0]

    def spans(frame):
        begin = jnp.max(jnp.where(starts[:, None] <= frame[None], starts[:, None], 0), 0)
        end = jnp.min(jnp.where(ends[:, None] > frame[None], ends[:, None], LEN), 0)
        return begin, end

    begin, end = spans(y * CHUNK + jnp.arange(CHUNK, dtype=jnp.int32))
    span = jnp.concatenate([begin[None], end[None], jnp.zeros((6, CHUNK), jnp.int32)], 0)
    firsts, lasts = slice(0, None, QT), slice(QT - 1, None, QT)
    scal = jnp.stack([begin[firsts], end[firsts], begin[lasts], end[lasts]], 1).reshape(-1)

    both = jnp.concatenate([w_out, w_glu[:, :D], w_glu[:, D:]], axis=0)
    late = ring[3][0, 0].astype(F32)
    w0 = jnp.where(late == jnp.inf, jnp.zeros_like(both), both)
    half = lax.dynamic_slice_in_dim(w0, c * 120, 120)
    w1 = along_z(w0)
    common = (q, span, scal)

    up, down = shift(kv, "y", 4, 1), shift(kv, "y", 4, -1)
    kv, w1 = tie(kv, w1)
    w2, far_half = along_z(w1), shift(half, "z", 8, 4)
    x0, x1, w1c = along_x(w0), along_x(w1), between_cores(w1)
    state = attend(((0, 0, 1024),), *common, (kv,), None, False, 1)

    up, down, w2, x0, x1, w1c, far_half, *state = tie(
        up, down, w2, x0, x1, w1c, far_half, *state
    )
    far0, far1 = shift(up[:512], "y", 4, 1), shift(down[512:], "y", 4, -1)
    w3, x2, w2c, x1c = along_z(w2), along_x(w2), between_cores(w2), between_cores(x1)
    x_half, far_halfc = along_x(far_half), between_cores(far_half)
    state = attend(((-1, 0, 1024),), *common, (up,), state, False, 1)
    state = attend(((1, 0, 1024),), *common, (down,), state, False, 1)

    far0, far1, w3, x2, w2c, x1c, x_half, far_halfc, *state = tie(
        far0, far1, w3, x2, w2c, x1c, x_half, far_halfc, *state
    )
    x3, w3c, x2c, x_halfc = [
        f(v)
        for f, v in (
            (along_x, w3), (between_cores, w3), (between_cores, x2), (between_cores, x_half)
        )
    ]
    out = attend(((-2, 0, 512), (2, 512, 512)), *common, (far0, far1), state, True, 1)
    x3c = between_cores(x3)

    def whole(mine, other):
        low, high = jnp.where(c == 0, mine, other), jnp.where(c == 0, other, mine)
        return jnp.concatenate([low, high], 0)

    w4, x4 = whole(far_half, far_halfc), whole(x_half, x_halfc)
    weights = [w0, w1, w2, w3, w4, w1c, w2c, w3c, x0, x1, x2, x3, x4, x1c, x2c, x3c]

    pieces = out.reshape(GROUP, ROWS, 256)
    attended = [lax.dynamic_index_in_dim(pieces, group, 0, keepdims=False)]
    for r in (1, 2, 3):
        sent = lax.dynamic_index_in_dim(pieces, group ^ r, 0, keepdims=False)
        attended.append(swap(sent, ("xh", "c"), r, 4))
    resid, gated = glu(attended, local, ln_conv_gain[None], weights)

    seq = ("y", "xh", "c")
    below = lax.ppermute(gated[ROWS - HALF :], seq, [(i, i + 1) for i in range(15)])
    above = lax.ppermute(gated[:HALF], seq, [(i + 1, i) for i in range(15)])
    frame = first_frame + jnp.arange(ROWS, dtype=jnp.int32)
    begin, end = spans(frame)
    taps = jnp.stack([begin - frame + HALF, end - frame + HALF], 0)
    blocks = slice(0, None, RB), slice(RB - 1, None, RB)
    plain = jnp.logical_and(
        begin[blocks[1]] <= frame[blocks[0]] - HALF, end[blocks[0]] >= frame[blocks[1]] + HALF
    ).astype(jnp.int32)
    taps = jnp.broadcast_to(taps[:, :, None], (2, ROWS, 128))
    dw = jnp.transpose(dw_kernel.reshape(CONV_K, TILES, 128), (1, 0, 2))
    return conv(plain, gated, below, above, taps, dw, ln_mid_gain[None], resid)[None]


def solution(mesh):
    fine = Mesh(mesh.devices.reshape(8, 2, 4, 2, 2), ("z", "xl", "y", "xh", "c"))
    dp, seq = ("z", "xl"), ("y", "xh", "c")
    return jax.shard_map(
        body,
        mesh=fine,
        in_specs=(
            P(dp, seq, None),
            P(dp, seq),
            P(),
            P(dp, None),
            P(dp, None),
            P(),
            P(dp, None),
            P(),
            P(),
        ),
        out_specs=P(dp, seq, None),
        check_vma=False,
    )
```

```python
import functools

import jax
import jax.numpy as jnp
from jax import lax
from jax.experimental import pallas as pl
from jax.experimental.pallas import tpu as pltpu
from jax.sharding import Mesh
from jax.sharding import PartitionSpec as P

D = 1536
HEADS = 12
HD = 64
CONV_K = 32
HALF = CONV_K // 2
IDS = 12
WIDTH = HEADS * HD
ROWS = 256
GROUP = 4
CHUNK = GROUP * ROWS
HCOLS = WIDTH // GROUP
LEN = 4096
KB = 512
QT = 512
NEG = -1e30
F32, BF16 = jnp.float32, jnp.bfloat16
ANY = pl.BlockSpec(memory_space=pl.ANY)
VM = pl.BlockSpec(memory_space=pltpu.VMEM)
SM = pl.BlockSpec(memory_space=pltpu.SMEM)


def params(limit_mib):
    return pltpu.CompilerParams(vmem_limit_bytes=limit_mib << 20)


def cost(us):
    return pl.CostEstimate(flops=int(us * 9e8), bytes_accessed=int(us * 2e6), transcendentals=0)


def shift(value, axis, count, step):
    return lax.ppermute(value, axis, [(i, (i + step) % count) for i in range(count)])


def swap(value, axes, mask, count):
    return lax.ppermute(value, axes, [(i, i ^ mask) for i in range(count)])


def along_z(value):
    pairs = []
    for i in range(8):
        pairs += [(2 * i, (i + 1) % 8 * 2), (2 * i + 1, (i + 7) % 8 * 2 + 1)]
    return lax.ppermute(value, ("z", "c"), pairs)


def along_x(value):
    def index(x, c):
        return x % 2 * 4 + x // 2 * 2 + c

    pairs = []
    for x in range(4):
        pairs += [(index(x, 0), index((x + 1) % 4, 0)), (index(x, 1), index((x + 3) % 4, 1))]
    return lax.ppermute(value, ("xl", "xh", "c"), pairs)


def tie(value, other):
    return lax.optimization_barrier((value, other))


def between_cores(value):
    return lax.ppermute(value, "c", [(0, 1), (1, 0)])


def norm(values, gain):
    centre = jnp.mean(values, -1, keepdims=True)
    shifted = values - centre
    spread = jnp.mean(shifted * shifted, -1, keepdims=True)
    return shifted * lax.rsqrt(spread + 1e-05) * gain


def z_owner(z, c, k, own):
    sign = (2 * c - 1) if own else (1 - 2 * c)
    return lax.rem(z + sign * k + 8, 8)


def qkv_kernel(n0, n1, n2, n3, *refs):
    srcs, (kv_ref, q_ref, w, sem) = refs[:8], refs[8:]
    z, xl, c = lax.axis_index("z"), lax.axis_index("xl"), lax.axis_index("c")
    me = lax.axis_index("xh") * 2 + c
    cols = pl.ds(pl.multiple_of(c * 640, 640), 640)
    copies = []
    for i, ref in enumerate(srcs):
        zz = z_owner(z, c, i, True) if i < 5 else z_owner(z, c, i - 4, False)
        for half in range(2):
            owner = zz * 2 + (xl if half == 0 else 1 - xl)
            rows = pl.ds(pl.multiple_of(owner * 96, 96), 96)
            copies.append(
                pltpu.make_async_copy(ref.at[pl.ds(half * 96, 96), cols], w.at[rows], sem)
            )
    for cp in copies:
        cp.start()
    for cp in copies:
        cp.wait()
    for r, ref in enumerate((n0, n1, n2, n3)):
        rows = pl.ds(pl.multiple_of((me ^ r) * ROWS, ROWS), ROWS)
        out = jnp.dot(ref[...], w[...], preferred_element_type=F32).astype(BF16)
        kv_ref[rows, :] = out[:, :384]
        q_ref[rows, :] = out[:, 384:]


def qkv(normed, srcs):
    return pl.pallas_call(
        qkv_kernel,
        name="qkv",
        out_shape=(
            jax.ShapeDtypeStruct((CHUNK, 384), BF16),
            jax.ShapeDtypeStruct((CHUNK, 256), BF16),
        ),
        in_specs=[VM] * 4 + [ANY] * 8,
        out_specs=(VM, VM),
        scratch_shapes=[pltpu.VMEM((D, 640), BF16), pltpu.SemaphoreType.DMA],
        compiler_params=params(12),
        cost_estimate=cost(5),
    )(*normed, *srcs)


def attn_kernel(parts, first, last, scal, q_ref, span, *refs):
    kvs, refs = refs[: len(parts)], refs[len(parts) :]
    if first:
        outs, (qs, vt, m, l, acc) = refs[:-5], refs[-5:]
    else:
        (ml_in, acc_in), outs, (qs, vt, m, l, acc) = refs[:2], refs[2:-5], refs[-5:]
    y = lax.axis_index("y")
    tile = pl.program_id(0)
    offs = [sum(p[2] for p in parts[:i]) // KB for i in range(len(parts))]

    @pl.when(tile == 0)
    def _():
        for kv, off, (_, _, count) in zip(kvs, offs, parts):
            for i in range(count // KB):
                rows = slice(i * KB, (i + 1) * KB)
                vt[off + i, :128] = kv[rows, 256:].T
                vt[off + i, 128:] = kv[rows, 128:256].T[:HD]

    low = lax.broadcasted_iota(jnp.int32, (QT, 128), 1) < HD
    qa, qb = q_ref[:, :128] * BF16(0.125), q_ref[:, 128:] * BF16(0.125)
    zero = jnp.zeros_like(qa)
    qs[0] = jnp.where(low, qa, zero)
    qs[1] = jnp.where(low, zero, qa)
    qs[2] = qb
    if first:
        m[...] = jnp.full_like(m, NEG)
        l[...] = jnp.zeros_like(l)
        acc[...] = jnp.zeros_like(acc)
    else:
        m[...] = ml_in[:8]
        l[...] = ml_in[8:]
        acc[...] = acc_in[...]
    s_first, e_first, s_last, e_last = [scal[tile * 4 + i] for i in range(4)]

    def step(kv, row, block, base, masked):
        if masked:
            frame = lax.broadcasted_iota(jnp.int32, (KB, QT), 0) + base
            keep = jnp.logical_and(frame >= span[0:1, :], frame < span[1:2, :])
        scores = [
            lax.dot_general(
                kv[pl.ds(row, KB), :128] if h < 2 else kv[pl.ds(row, KB), 128:256],
                qs[h],
                (((1,), (1,)), ((), ())),
                preferred_element_type=F32,
            )
            for h in range(3)
        ]
        for h in range(3):
            s = jnp.where(keep, scores[h], NEG) if masked else scores[h]
            old = m[h : h + 1]
            new = jnp.maximum(old, jnp.max(s, axis=0, keepdims=True))
            p = jnp.exp(s - new)
            alpha = jnp.exp(old - new)
            m[h : h + 1] = new
            l[h : h + 1] = alpha * l[h : h + 1] + jnp.sum(p, axis=0, keepdims=True)
            rows = slice(h * HD, (h + 1) * HD)
            pv = jnp.dot(vt[block, rows], p.astype(BF16), preferred_element_type=F32)
            acc[rows] = alpha * acc[rows] + pv

    for kv, block, (off, start, count) in zip(kvs, offs, parts):
        begin = lax.rem(y + off + 4, 4) * CHUNK + start
        low_i = jnp.clip(lax.div(jnp.maximum(s_first - begin, 0), KB), 0, count // KB)
        high_i = jnp.clip(lax.div(jnp.maximum(e_last - begin, 0) + KB - 1, KB), 0, count // KB)

        @pl.loop(low_i, high_i)
        def _(i):
            base = begin + i * KB
            row = pl.multiple_of(i * KB, KB)
            plain = jnp.logical_and(s_last <= base, e_first >= base + KB)

            @pl.when(plain)
            def _():
                step(kv, row, block + i, base, False)

            @pl.when(jnp.logical_not(plain))
            def _():
                step(kv, row, block + i, base, True)

    if last:
        (out,) = outs
        for h in range(3):
            rows = slice(h * HD, (h + 1) * HD)
            acc[rows] = acc[rows] / l[h : h + 1]
        out[:, :128] = acc[:128].T.astype(BF16)
        tail = jnp.concatenate([acc[128:], jnp.zeros((HD, QT), F32)], 0)
        out[:, 128:] = tail.T.astype(BF16)
    else:
        ml_out, acc_out = outs
        ml_out[:8] = m[...]
        ml_out[8:] = l[...]
        acc_out[...] = acc[...]


def attend(parts, q, span, scal, kvs, state, last, us):
    first = state is None

    def rows(count):
        return pl.BlockSpec((QT, count), lambda i: (i, 0))

    def cols(count):
        return pl.BlockSpec((count, QT), lambda i: (0, i))

    state_shapes = (
        jax.ShapeDtypeStruct((16, CHUNK), F32),
        jax.ShapeDtypeStruct((HCOLS, CHUNK), F32),
    )
    return pl.pallas_call(
        functools.partial(attn_kernel, parts, first, last),
        name="attend",
        grid=(CHUNK // QT,),
        out_shape=jax.ShapeDtypeStruct((CHUNK, 256), BF16) if last else state_shapes,
        in_specs=[SM, rows(256), cols(8)]
        + [VM] * len(kvs)
        + ([] if first else [cols(16), cols(HCOLS)]),
        out_specs=rows(256) if last else (cols(16), cols(HCOLS)),
        scratch_shapes=[
            pltpu.VMEM((3, QT, 128), BF16),
            pltpu.VMEM((sum(p[2] for p in parts) // KB, HCOLS, KB), BF16),
            pltpu.VMEM((8, QT), F32),
            pltpu.VMEM((8, QT), F32),
            pltpu.VMEM((HCOLS, QT), F32),
        ],
        compiler_params=params(18),
        cost_estimate=cost(us),
    )(scal, q, span, *kvs, *(() if first else state))


def glu_kernel(a0, a1, a2, a3, local, gain, *refs):
    srcs, (resid_ref, gated_ref, wo, wv, wg, sem_o, sem_g) = refs[:16], refs[16:]
    z, xl, c = lax.axis_index("z"), lax.axis_index("xl"), lax.axis_index("c")
    me = lax.axis_index("xh") * 2 + c
    out_copies, glu_copies = [], []

    def rows(owner, count):
        return pl.ds(pl.multiple_of(owner * count, count), count)

    for half in range(2):
        for i in range(8):
            ref = srcs[8 * half + i]
            zz = z_owner(z, c, i, True) if i < 5 else z_owner(z, c, i - 4, False)
            owner = zz * 2 + (xl if half == 0 else 1 - xl)
            out_copies.append(
                pltpu.make_async_copy(ref.at[pl.ds(0, 48)], wo.at[rows(owner, 48)], sem_o)
            )
            glu_copies.append(
                pltpu.make_async_copy(ref.at[pl.ds(48, 96)], wv.at[rows(owner, 96)], sem_g)
            )
            glu_copies.append(
                pltpu.make_async_copy(ref.at[pl.ds(144, 96)], wg.at[rows(owner, 96)], sem_g)
            )
    for cp in out_copies + glu_copies:
        cp.start()
    for cp in out_copies:
        cp.wait()
    attn = jnp.zeros((ROWS, D), F32)
    for r, ref in enumerate((a0, a1, a2, a3)):
        part = wo[rows(me ^ r, HCOLS), :]
        attn = attn + jnp.dot(ref[:, :HCOLS], part, preferred_element_type=F32)
    resid = (local[...].astype(F32) + attn).astype(BF16)
    resid_ref[...] = resid
    glu_in = norm(resid.astype(F32), gain[...]).astype(BF16)
    for cp in glu_copies:
        cp.wait()
    for j in range(0, D, 512):
        value = jnp.dot(glu_in, wv[:, j : j + 512], preferred_element_type=F32)
        gate = jnp.dot(glu_in, wg[:, j : j + 512], preferred_element_type=F32)
        gated_ref[:, j : j + 512] = (value * jax.nn.sigmoid(gate)).astype(BF16)


def glu(attended, local, gain, srcs):
    return pl.pallas_call(
        glu_kernel,
        name="glu",
        out_shape=(jax.ShapeDtypeStruct((ROWS, D), BF16),) * 2,
        in_specs=[VM] * 6 + [ANY] * 16,
        out_specs=(VM, VM),
        scratch_shapes=[
            pltpu.VMEM((WIDTH, D), BF16),
            pltpu.VMEM((D, D), BF16),
            pltpu.VMEM((D, D), BF16),
            pltpu.SemaphoreType.DMA,
            pltpu.SemaphoreType.DMA,
        ],
        compiler_params=params(26),
        cost_estimate=cost(10),
    )(*attended, local, gain, *srcs)


RB = 32
CT = 4
TILES = D // 128


def conv_kernel(scal, gated, below, above, taps, dw, gain, resid, out, xb, cv):
    for t in range(TILES):
        cols = slice(t * 128, (t + 1) * 128)
        xb[t, :HALF] = below[:, cols].astype(F32)
        xb[t, HALF : HALF + ROWS] = gated[:, cols].astype(F32)
        xb[t, HALF + ROWS :] = above[:, cols].astype(F32)

    def block(r0, group, masked):
        total = [jnp.zeros((RB, 128), F32) for _ in range(CT)]
        if masked:
            begin, end = taps[0, pl.ds(r0, RB), :], taps[1, pl.ds(r0, RB), :]
        for j in range(CONV_K):
            if masked:
                keep = jnp.logical_and(begin <= j, j < end)
            for t in range(CT):
                tile = group * CT + t
                term = xb[tile, pl.ds(r0 + j, RB), :] * dw[tile, j : j + 1, :]
                total[t] = total[t] + (jnp.where(keep, term, 0.0) if masked else term)
        for t in range(CT):
            cv[group * CT + t, pl.ds(r0, RB), :] = total[t]

    @pl.loop(0, ROWS // RB)
    def _(i):
        r0 = pl.multiple_of(i * RB, RB)

        @pl.loop(0, TILES // CT)
        def _(group):
            @pl.when(scal[i] == 1)
            def _():
                block(r0, group, False)

            @pl.when(scal[i] == 0)
            def _():
                block(r0, group, True)

    @pl.loop(0, ROWS // 64)
    def _(i):
        rows = pl.ds(pl.multiple_of(i * 64, 64), 64)
        parts = [cv[t, rows, :] for t in range(TILES)]
        centre = jnp.sum(sum(parts), -1, keepdims=True) * (1.0 / D)
        parts = [p - centre for p in parts]
        spread = jnp.sum(sum(p * p for p in parts), -1, keepdims=True) * (1.0 / D)
        scale = lax.rsqrt(spread + 1e-05)
        for t in range(TILES):
            cols = slice(t * 128, (t + 1) * 128)
            mid = parts[t] * scale * gain[:, cols]
            res = resid[rows, cols].astype(F32)
            out[rows, cols] = (res + mid * jax.nn.sigmoid(mid)).astype(BF16)


def conv(scal, gated, below, above, taps, dw, gain, resid):
    return pl.pallas_call(
        conv_kernel,
        name="conv",
        out_shape=jax.ShapeDtypeStruct((ROWS, D), BF16),
        in_specs=[SM] + [VM] * 7,
        out_specs=VM,
        scratch_shapes=[
            pltpu.VMEM((TILES, ROWS + CONV_K, 128), F32),
            pltpu.VMEM((TILES, ROWS, 128), F32),
        ],
        compiler_params=params(14),
        cost_estimate=cost(8),
    )(scal, gated, below, above, taps, dw, gain, resid)


def body(
    frames, segment_ids, ln_attn_gain, w_qkv, w_out, ln_conv_gain, w_glu, dw_kernel, ln_mid_gain
):
    local = frames[0]
    y, xh, c = lax.axis_index("y"), lax.axis_index("xh"), lax.axis_index("c")
    group = xh * 2 + c
    first_frame = (y * GROUP + group) * ROWS

    wq, wk, wv = [
        lax.dynamic_slice_in_dim(w_qkv, part * WIDTH + xh * 2 * HCOLS, 2 * HCOLS, 1)
        for part in range(3)
    ]
    columns = []
    for j in (0, HCOLS):
        columns += [wk[:, j : j + 128], wv[:, j + 128 : j + HCOLS], wk[:, j + 128 : j + HCOLS]]
        columns += [wv[:, j : j + 128], wq[:, j : j + 128], jnp.zeros((96, HD), BF16)]
        columns += [wq[:, j + 128 : j + HCOLS]]
    own = jnp.concatenate(columns, axis=1)
    ids = lax.broadcasted_iota(jnp.int32, (IDS, ROWS), 0)
    counts = jnp.sum((segment_ids == ids).astype(jnp.int32), axis=1)[None]
    hops = (("c", 1, 2), ("xh", 1, 2), ("y", 1, 4), ("y", 2, 4))
    ring = [jnp.concatenate([own, swap(own, "xl", 1, 2)], axis=0)]
    for axis, mask, count in hops:
        counts = counts + swap(counts, axis, mask, count)
        src, counts = tie(ring[-1], counts)
        ring.append(along_z(src))
    srcs = ring + [between_cores(v) for v in ring[1:4]]

    normed = norm(local.astype(F32), ln_attn_gain).astype(BF16)
    n2, srcs[3] = tie(swap(normed, "xh", 1, 2), ring[3])
    pieces = [normed, between_cores(normed), n2, between_cores(n2)]
    kv, q = qkv(pieces, srcs)

    ends = jnp.cumsum(counts[0])
    starts = ends - counts[0]

    def spans(frame):
        begin = jnp.max(jnp.where(starts[:, None] <= frame[None], starts[:, None], 0), 0)
        end = jnp.min(jnp.where(ends[:, None] > frame[None], ends[:, None], LEN), 0)
        return begin, end

    begin, end = spans(y * CHUNK + jnp.arange(CHUNK, dtype=jnp.int32))
    span = jnp.concatenate([begin[None], end[None], jnp.zeros((6, CHUNK), jnp.int32)], 0)
    firsts, lasts = slice(0, None, QT), slice(QT - 1, None, QT)
    scal = jnp.stack([begin[firsts], end[firsts], begin[lasts], end[lasts]], 1).reshape(-1)

    both = jnp.concatenate([w_out, w_glu[:, :D], w_glu[:, D:]], axis=0)
    late = ring[3][0, 0].astype(F32)
    w0 = jnp.where(late == jnp.inf, jnp.zeros_like(both), both)
    w1 = along_z(w0)
    src, kv_later = tie(w1, kv)
    w2 = along_z(src)
    up, down = shift(kv, "y", 4, 1), shift(kv, "y", 4, -1)
    common = (q, span, scal)
    kv, w1_later = tie(kv_later, w1)
    state = attend(((0, 0, 1024),), *common, (kv,), None, False, 7)
    src, mark = tie(w2, state[0])
    w3 = along_z(src)
    w4 = along_z(w3)
    far_src, mark = tie((up[:512], down[512:]), mark)
    far0, far1 = shift(far_src[0], "y", 4, 1), shift(far_src[1], "y", 4, -1)
    up, w2_later = tie(up, w2)
    down, w3_later = tie(down, w3)
    far0, w4_later = tie(far0, w4)
    z_set = [w0, w1_later, w2_later, w3_later, w4_later]
    x_set = [along_x(v) for v in (w0, w1, w2, w3, w4)]
    weights = []
    for values in (z_set, x_set):
        weights += values + [between_cores(v) for v in values[1:4]]
    state = attend(((-1, 0, 1024),), *common, (up,), (mark, state[1]), False, 10)
    state = attend(((1, 0, 1024),), *common, (down,), state, False, 14)
    out = attend(((-2, 0, 512), (2, 512, 512)), *common, (far0, far1), state, True, 7)

    pieces = out.reshape(GROUP, ROWS, 256)
    attended = [lax.dynamic_index_in_dim(pieces, group, 0, keepdims=False)]
    for r in (1, 2, 3):
        sent = lax.dynamic_index_in_dim(pieces, group ^ r, 0, keepdims=False)
        attended.append(swap(sent, ("xh", "c"), r, 4))
    resid, gated = glu(attended, local, ln_conv_gain[None], weights)

    seq = ("y", "xh", "c")
    below = lax.ppermute(gated[ROWS - HALF :], seq, [(i, i + 1) for i in range(15)])
    above = lax.ppermute(gated[:HALF], seq, [(i + 1, i) for i in range(15)])
    frame = first_frame + jnp.arange(ROWS, dtype=jnp.int32)
    begin, end = spans(frame)
    taps = jnp.stack([begin - frame + HALF, end - frame + HALF], 0)
    blocks = slice(0, None, RB), slice(RB - 1, None, RB)
    plain = jnp.logical_and(
        begin[blocks[1]] <= frame[blocks[0]] - HALF, end[blocks[0]] >= frame[blocks[1]] + HALF
    ).astype(jnp.int32)
    taps = jnp.broadcast_to(taps[:, :, None], (2, ROWS, 128))
    dw = jnp.transpose(dw_kernel.reshape(CONV_K, TILES, 128), (1, 0, 2))
    return conv(plain, gated, below, above, taps, dw, ln_mid_gain[None], resid)[None]


def solution(mesh):
    fine = Mesh(mesh.devices.reshape(8, 2, 4, 2, 2), ("z", "xl", "y", "xh", "c"))
    dp, seq = ("z", "xl"), ("y", "xh", "c")
    return jax.shard_map(
        body,
        mesh=fine,
        in_specs=(
            P(dp, seq, None),
            P(dp, seq),
            P(),
            P(dp, None),
            P(dp, None),
            P(),
            P(dp, None),
            P(),
            P(),
        ),
        out_specs=P(dp, seq, None),
        check_vma=False,
    )
```

```python
import functools

import jax
import jax.numpy as jnp
from jax import lax
from jax.experimental import pallas as pl
from jax.experimental.pallas import tpu as pltpu
from jax.sharding import Mesh
from jax.sharding import PartitionSpec as P

D = 1536
HEADS = 12
HD = 64
CONV_K = 32
HALF = CONV_K // 2
IDS = 12
WIDTH = HEADS * HD
ROWS = 256
GROUP = 4
CHUNK = GROUP * ROWS
HCOLS = WIDTH // GROUP
LEN = 4096
KB = 512
QT = 512
NEG = -1e30
F32, BF16 = jnp.float32, jnp.bfloat16
ANY = pl.BlockSpec(memory_space=pl.ANY)
VM = pl.BlockSpec(memory_space=pltpu.VMEM)
SM = pl.BlockSpec(memory_space=pltpu.SMEM)


def params(limit_mib):
    return pltpu.CompilerParams(vmem_limit_bytes=limit_mib << 20)


def cost(us):
    return pl.CostEstimate(flops=int(us * 9e8), bytes_accessed=int(us * 2e6), transcendentals=0)


def shift(value, axis, count, step):
    return lax.ppermute(value, axis, [(i, (i + step) % count) for i in range(count)])


def swap(value, axes, mask, count):
    return lax.ppermute(value, axes, [(i, i ^ mask) for i in range(count)])


def along_z(value):
    pairs = []
    for i in range(8):
        pairs += [(2 * i, (i + 1) % 8 * 2), (2 * i + 1, (i + 7) % 8 * 2 + 1)]
    return lax.ppermute(value, ("z", "c"), pairs)


def along_x(value):
    def index(x, c):
        return x % 2 * 4 + x // 2 * 2 + c

    pairs = []
    for x in range(4):
        pairs += [(index(x, 0), index((x + 1) % 4, 0)), (index(x, 1), index((x + 3) % 4, 1))]
    return lax.ppermute(value, ("xl", "xh", "c"), pairs)


def tie(value, other):
    return lax.optimization_barrier((value, other))


def between_cores(value):
    return lax.ppermute(value, "c", [(0, 1), (1, 0)])


def norm(values, gain):
    centre = jnp.mean(values, -1, keepdims=True)
    shifted = values - centre
    spread = jnp.mean(shifted * shifted, -1, keepdims=True)
    return shifted * lax.rsqrt(spread + 1e-05) * gain


def z_owner(z, c, k, own):
    sign = (2 * c - 1) if own else (1 - 2 * c)
    return lax.rem(z + sign * k + 8, 8)


def qkv_kernel(n0, n1, n2, n3, *refs):
    srcs, (kv_ref, q_ref, w, sem) = refs[:8], refs[8:]
    z, xl, c = lax.axis_index("z"), lax.axis_index("xl"), lax.axis_index("c")
    me = lax.axis_index("xh") * 2 + c
    cols = pl.ds(pl.multiple_of(c * 640, 640), 640)
    copies = []
    for i, ref in enumerate(srcs):
        zz = z_owner(z, c, i, True) if i < 5 else z_owner(z, c, i - 4, False)
        for half in range(2):
            owner = zz * 2 + (xl if half == 0 else 1 - xl)
            rows = pl.ds(pl.multiple_of(owner * 96, 96), 96)
            copies.append(
                pltpu.make_async_copy(ref.at[pl.ds(half * 96, 96), cols], w.at[rows], sem)
            )
    for cp in copies:
        cp.start()
    for cp in copies:
        cp.wait()
    for r, ref in enumerate((n0, n1, n2, n3)):
        rows = pl.ds(pl.multiple_of((me ^ r) * ROWS, ROWS), ROWS)
        out = jnp.dot(ref[...], w[...], preferred_element_type=F32).astype(BF16)
        kv_ref[rows, :] = out[:, :384]
        q_ref[rows, :] = out[:, 384:]


def qkv(normed, srcs):
    return pl.pallas_call(
        qkv_kernel,
        name="qkv",
        out_shape=(
            jax.ShapeDtypeStruct((CHUNK, 384), BF16),
            jax.ShapeDtypeStruct((CHUNK, 256), BF16),
        ),
        in_specs=[VM] * 4 + [ANY] * 8,
        out_specs=(VM, VM),
        scratch_shapes=[pltpu.VMEM((D, 640), BF16), pltpu.SemaphoreType.DMA],
        compiler_params=params(12),
        cost_estimate=cost(5),
    )(*normed, *srcs)


def attn_kernel(parts, first, last, scal, q_ref, span, *refs):
    kvs, refs = refs[: len(parts)], refs[len(parts) :]
    if first:
        outs, (qs, vt, m, l, acc) = refs[:-5], refs[-5:]
    else:
        (ml_in, acc_in), outs, (qs, vt, m, l, acc) = refs[:2], refs[2:-5], refs[-5:]
    y = lax.axis_index("y")
    tile = pl.program_id(0)
    offs = [sum(p[2] for p in parts[:i]) // KB for i in range(len(parts))]

    @pl.when(tile == 0)
    def _():
        for kv, off, (_, _, count) in zip(kvs, offs, parts):
            for i in range(count // KB):
                rows = slice(i * KB, (i + 1) * KB)
                vt[off + i, :128] = kv[rows, 256:].T
                vt[off + i, 128:] = kv[rows, 128:256].T[:HD]

    low = lax.broadcasted_iota(jnp.int32, (QT, 128), 1) < HD
    qa, qb = q_ref[:, :128] * BF16(0.125), q_ref[:, 128:] * BF16(0.125)
    zero = jnp.zeros_like(qa)
    qs[0] = jnp.where(low, qa, zero)
    qs[1] = jnp.where(low, zero, qa)
    qs[2] = qb
    if first:
        m[...] = jnp.full_like(m, NEG)
        l[...] = jnp.zeros_like(l)
        acc[...] = jnp.zeros_like(acc)
    else:
        m[...] = ml_in[:8]
        l[...] = ml_in[8:]
        acc[...] = acc_in[...]
    s_first, e_first, s_last, e_last = [scal[tile * 4 + i] for i in range(4)]

    def step(kv, row, block, base, masked):
        if masked:
            frame = lax.broadcasted_iota(jnp.int32, (KB, QT), 0) + base
            keep = jnp.logical_and(frame >= span[0:1, :], frame < span[1:2, :])
        scores = [
            lax.dot_general(
                kv[pl.ds(row, KB), :128] if h < 2 else kv[pl.ds(row, KB), 128:256],
                qs[h],
                (((1,), (1,)), ((), ())),
                preferred_element_type=F32,
            )
            for h in range(3)
        ]
        for h in range(3):
            s = jnp.where(keep, scores[h], NEG) if masked else scores[h]
            old = m[h : h + 1]
            new = jnp.maximum(old, jnp.max(s, axis=0, keepdims=True))
            p = jnp.exp(s - new)
            alpha = jnp.exp(old - new)
            m[h : h + 1] = new
            l[h : h + 1] = alpha * l[h : h + 1] + jnp.sum(p, axis=0, keepdims=True)
            rows = slice(h * HD, (h + 1) * HD)
            pv = jnp.dot(vt[block, rows], p.astype(BF16), preferred_element_type=F32)
            acc[rows] = alpha * acc[rows] + pv

    for kv, block, (off, start, count) in zip(kvs, offs, parts):
        begin = lax.rem(y + off + 4, 4) * CHUNK + start
        low_i = jnp.clip(lax.div(jnp.maximum(s_first - begin, 0), KB), 0, count // KB)
        high_i = jnp.clip(lax.div(jnp.maximum(e_last - begin, 0) + KB - 1, KB), 0, count // KB)

        @pl.loop(low_i, high_i)
        def _(i):
            base = begin + i * KB
            row = pl.multiple_of(i * KB, KB)
            plain = jnp.logical_and(s_last <= base, e_first >= base + KB)

            @pl.when(plain)
            def _():
                step(kv, row, block + i, base, False)

            @pl.when(jnp.logical_not(plain))
            def _():
                step(kv, row, block + i, base, True)

    if last:
        (out,) = outs
        for h in range(3):
            rows = slice(h * HD, (h + 1) * HD)
            acc[rows] = acc[rows] / l[h : h + 1]
        out[:, :128] = acc[:128].T.astype(BF16)
        tail = jnp.concatenate([acc[128:], jnp.zeros((HD, QT), F32)], 0)
        out[:, 128:] = tail.T.astype(BF16)
    else:
        ml_out, acc_out = outs
        ml_out[:8] = m[...]
        ml_out[8:] = l[...]
        acc_out[...] = acc[...]


def attend(parts, q, span, scal, kvs, state, last, us):
    first = state is None

    def rows(count):
        return pl.BlockSpec((QT, count), lambda i: (i, 0))

    def cols(count):
        return pl.BlockSpec((count, QT), lambda i: (0, i))

    state_shapes = (
        jax.ShapeDtypeStruct((16, CHUNK), F32),
        jax.ShapeDtypeStruct((HCOLS, CHUNK), F32),
    )
    return pl.pallas_call(
        functools.partial(attn_kernel, parts, first, last),
        name="attend",
        grid=(CHUNK // QT,),
        out_shape=jax.ShapeDtypeStruct((CHUNK, 256), BF16) if last else state_shapes,
        in_specs=[SM, rows(256), cols(8)]
        + [VM] * len(kvs)
        + ([] if first else [cols(16), cols(HCOLS)]),
        out_specs=rows(256) if last else (cols(16), cols(HCOLS)),
        scratch_shapes=[
            pltpu.VMEM((3, QT, 128), BF16),
            pltpu.VMEM((sum(p[2] for p in parts) // KB, HCOLS, KB), BF16),
            pltpu.VMEM((8, QT), F32),
            pltpu.VMEM((8, QT), F32),
            pltpu.VMEM((HCOLS, QT), F32),
        ],
        compiler_params=params(18),
        cost_estimate=cost(us),
    )(scal, q, span, *kvs, *(() if first else state))


def glu_kernel(a0, a1, a2, a3, local, gain, *refs):
    srcs, (resid_ref, gated_ref, wo, wv, wg, sem_o, sem_g) = refs[:16], refs[16:]
    z, xl, c = lax.axis_index("z"), lax.axis_index("xl"), lax.axis_index("c")
    me = lax.axis_index("xh") * 2 + c
    out_copies, glu_copies = [], []

    def rows(owner, count):
        return pl.ds(pl.multiple_of(owner * count, count), count)

    for half in range(2):
        for i in range(8):
            ref = srcs[8 * half + i]
            zz = z_owner(z, c, i, True) if i < 5 else z_owner(z, c, i - 4, False)
            owner = zz * 2 + (xl if half == 0 else 1 - xl)
            out_copies.append(
                pltpu.make_async_copy(ref.at[pl.ds(0, 48)], wo.at[rows(owner, 48)], sem_o)
            )
            glu_copies.append(
                pltpu.make_async_copy(ref.at[pl.ds(48, 96)], wv.at[rows(owner, 96)], sem_g)
            )
            glu_copies.append(
                pltpu.make_async_copy(ref.at[pl.ds(144, 96)], wg.at[rows(owner, 96)], sem_g)
            )
    for cp in out_copies + glu_copies:
        cp.start()
    for cp in out_copies:
        cp.wait()
    attn = jnp.zeros((ROWS, D), F32)
    for r, ref in enumerate((a0, a1, a2, a3)):
        part = wo[rows(me ^ r, HCOLS), :]
        attn = attn + jnp.dot(ref[:, :HCOLS], part, preferred_element_type=F32)
    resid = (local[...].astype(F32) + attn).astype(BF16)
    resid_ref[...] = resid
    glu_in = norm(resid.astype(F32), gain[...]).astype(BF16)
    for cp in glu_copies:
        cp.wait()
    for j in range(0, D, 512):
        value = jnp.dot(glu_in, wv[:, j : j + 512], preferred_element_type=F32)
        gate = jnp.dot(glu_in, wg[:, j : j + 512], preferred_element_type=F32)
        gated_ref[:, j : j + 512] = (value * jax.nn.sigmoid(gate)).astype(BF16)


def glu(attended, local, gain, srcs):
    return pl.pallas_call(
        glu_kernel,
        name="glu",
        out_shape=(jax.ShapeDtypeStruct((ROWS, D), BF16),) * 2,
        in_specs=[VM] * 6 + [ANY] * 16,
        out_specs=(VM, VM),
        scratch_shapes=[
            pltpu.VMEM((WIDTH, D), BF16),
            pltpu.VMEM((D, D), BF16),
            pltpu.VMEM((D, D), BF16),
            pltpu.SemaphoreType.DMA,
            pltpu.SemaphoreType.DMA,
        ],
        compiler_params=params(26),
        cost_estimate=cost(10),
    )(*attended, local, gain, *srcs)


RB = 32
CT = 4
TILES = D // 128


def conv_block(i, scal, taps, dw, xb, cv, x0, c0):
    r0 = pl.multiple_of(i * RB, RB)

    def block(group, masked):
        total = [jnp.zeros((RB, 128), F32) for _ in range(CT)]
        if masked:
            begin, end = taps[0, pl.ds(r0, RB), :], taps[1, pl.ds(r0, RB), :]
        for j in range(CONV_K):
            if masked:
                keep = jnp.logical_and(begin <= j, j < end)
            for t in range(CT):
                tile = group * CT + t
                term = xb[tile, pl.ds(x0 + j, RB), :] * dw[tile, j : j + 1, :]
                total[t] = total[t] + (jnp.where(keep, term, 0.0) if masked else term)
        for t in range(CT):
            cv[group * CT + t, pl.ds(c0, RB), :] = total[t]

    @pl.loop(0, TILES // CT)
    def _(group):
        @pl.when(scal[i] == 1)
        def _():
            block(group, False)

        @pl.when(scal[i] == 0)
        def _():
            block(group, True)


def finish(cv, cv_rows, gain, resid, resid_rows, out, out_rows):
    parts = [cv[t, cv_rows, :] for t in range(TILES)]
    centre = jnp.sum(sum(parts), -1, keepdims=True) * (1.0 / D)
    parts = [p - centre for p in parts]
    spread = jnp.sum(sum(p * p for p in parts), -1, keepdims=True) * (1.0 / D)
    scale = lax.rsqrt(spread + 1e-05)
    for t in range(TILES):
        cols = slice(t * 128, (t + 1) * 128)
        mid = parts[t] * scale * gain[:, cols]
        res = resid[resid_rows, cols].astype(F32)
        out[out_rows, cols] = (res + mid * jax.nn.sigmoid(mid)).astype(BF16)


def inner_kernel(scal, gated, taps, dw, gain, resid, out, xb, cv):
    for t in range(TILES):
        xb[t] = gated[:, t * 128 : (t + 1) * 128].astype(F32)

    @pl.loop(1, ROWS // RB - 1)
    def _(i):
        r0 = pl.multiple_of(i * RB, RB)
        conv_block(i, scal, taps, dw, xb, cv, r0 - HALF, r0)

    @pl.loop(0, (ROWS - 2 * RB) // 64)
    def _(i):
        rows = pl.ds(pl.multiple_of(RB + i * 64, RB), 64)
        finish(cv, rows, gain, resid, rows, out, rows)


def edge_kernel(scal, _, gated, below, above, taps, dw, gain, resid, out, xb, cv):
    part = pl.program_id(0)
    near = RB + HALF

    @pl.when(part == 0)
    def _():
        for t in range(TILES):
            cols = slice(t * 128, (t + 1) * 128)
            xb[t, :HALF] = below[:, cols].astype(F32)
            xb[t, HALF:] = gated[:near, cols].astype(F32)

    @pl.when(part == 1)
    def _():
        for t in range(TILES):
            cols = slice(t * 128, (t + 1) * 128)
            xb[t, :near] = gated[ROWS - near :, cols].astype(F32)
            xb[t, near:] = above[:, cols].astype(F32)

    block = part * (ROWS // RB - 1)
    conv_block(block, scal, taps, dw, xb, cv, 0, 0)
    rows = slice(0, RB)
    finish(cv, rows, gain, resid, pl.ds(pl.multiple_of(block * RB, RB), RB), out, rows)


def conv_inner(scal, gated, taps, dw, gain, resid):
    return pl.pallas_call(
        inner_kernel,
        name="inner",
        out_shape=jax.ShapeDtypeStruct((ROWS, D), BF16),
        in_specs=[SM] + [VM] * 5,
        out_specs=VM,
        scratch_shapes=[
            pltpu.VMEM((TILES, ROWS, 128), F32),
            pltpu.VMEM((TILES, ROWS, 128), F32),
        ],
        compiler_params=params(14),
        cost_estimate=cost(8),
    )(scal, gated, taps, dw, gain, resid)


def conv_edges(scal, inner, gated, below, above, taps, dw, gain, resid):
    return pl.pallas_call(
        edge_kernel,
        name="edges",
        grid=(2,),
        out_shape=jax.ShapeDtypeStruct((ROWS, D), BF16),
        in_specs=[SM, ANY] + [VM] * 7,
        out_specs=pl.BlockSpec((RB, D), lambda i: (i * (ROWS // RB - 1), 0)),
        scratch_shapes=[
            pltpu.VMEM((TILES, RB + CONV_K, 128), F32),
            pltpu.VMEM((TILES, RB, 128), F32),
        ],
        input_output_aliases={1: 0},
        compiler_params=params(14),
        cost_estimate=cost(3),
    )(scal, inner, gated, below, above, taps, dw, gain, resid)


def body(
    frames, segment_ids, ln_attn_gain, w_qkv, w_out, ln_conv_gain, w_glu, dw_kernel, ln_mid_gain
):
    local = frames[0]
    y, xh, c = lax.axis_index("y"), lax.axis_index("xh"), lax.axis_index("c")
    group = xh * 2 + c
    first_frame = (y * GROUP + group) * ROWS

    wq, wk, wv = [
        lax.dynamic_slice_in_dim(w_qkv, part * WIDTH + xh * 2 * HCOLS, 2 * HCOLS, 1)
        for part in range(3)
    ]
    columns = []
    for j in (0, HCOLS):
        columns += [wk[:, j : j + 128], wv[:, j + 128 : j + HCOLS], wk[:, j + 128 : j + HCOLS]]
        columns += [wv[:, j : j + 128], wq[:, j : j + 128], jnp.zeros((96, HD), BF16)]
        columns += [wq[:, j + 128 : j + HCOLS]]
    own = jnp.concatenate(columns, axis=1)
    ids = lax.broadcasted_iota(jnp.int32, (IDS, ROWS), 0)
    counts = jnp.sum((segment_ids == ids).astype(jnp.int32), axis=1)[None]
    hops = (("c", 1, 2), ("xh", 1, 2), ("y", 1, 4), ("y", 2, 4))
    ring = [jnp.concatenate([own, swap(own, "xl", 1, 2)], axis=0)]
    for step_hops in (hops[:1], hops[1:2], hops[2:], ()):
        src = ring[-1]
        for axis, mask, count in step_hops:
            counts = counts + swap(counts, axis, mask, count)
        if step_hops:
            src, counts = tie(src, counts)
        ring.append(along_z(src))
    srcs = ring + [between_cores(v) for v in ring[1:4]]

    normed = norm(local.astype(F32), ln_attn_gain).astype(BF16)
    n2, srcs[3] = tie(swap(normed, "xh", 1, 2), ring[3])
    pieces = [normed, between_cores(normed), n2, between_cores(n2)]
    kv, q = qkv(pieces, srcs)

    ends = jnp.cumsum(counts[0])
    starts = ends - counts[0]

    def spans(frame):
        begin = jnp.max(jnp.where(starts[:, None] <= frame[None], starts[:, None], 0), 0)
        end = jnp.min(jnp.where(ends[:, None] > frame[None], ends[:, None], LEN), 0)
        return begin, end

    begin, end = spans(y * CHUNK + jnp.arange(CHUNK, dtype=jnp.int32))
    span = jnp.concatenate([begin[None], end[None], jnp.zeros((6, CHUNK), jnp.int32)], 0)
    firsts, lasts = slice(0, None, QT), slice(QT - 1, None, QT)
    scal = jnp.stack([begin[firsts], end[firsts], begin[lasts], end[lasts]], 1).reshape(-1)

    both = jnp.concatenate([w_out, w_glu[:, :D], w_glu[:, D:]], axis=0)
    late = ring[3][0, 0].astype(F32)
    w0 = jnp.where(late == jnp.inf, jnp.zeros_like(both), both)
    w1 = along_z(w0)
    src, kv_later = tie(w1, kv)
    w2 = along_z(src)
    up, down = shift(kv, "y", 4, 1), shift(kv, "y", 4, -1)
    common = (q, span, scal)
    kv, w1_later = tie(kv_later, w1)
    state = attend(((0, 0, 1024),), *common, (kv,), None, False, 7)
    src, x1_src, mark = lax.optimization_barrier((w2, w1_later, state[0]))
    w3 = along_z(src)
    w4 = along_z(w3)
    far_src, mark = tie((up[:512], down[512:]), mark)
    far0, far1 = shift(far_src[0], "y", 4, 1), shift(far_src[1], "y", 4, -1)
    up, w2_later = tie(up, w2)
    down, w3_later = tie(down, w3)
    far0, w4_later = tie(far0, w4)
    z_set = [w0, w1_later, w2_later, w3_later, w4_later]
    x_set = [along_x(v) for v in (w0, x1_src, w2, w3, w4)]
    weights = []
    for values in (z_set, x_set):
        weights += values + [between_cores(v) for v in values[1:4]]
    state = attend(((-1, 0, 1024),), *common, (up,), (mark, state[1]), False, 10)
    state = attend(((1, 0, 1024),), *common, (down,), state, False, 14)
    out = attend(((-2, 0, 512), (2, 512, 512)), *common, (far0, far1), state, True, 7)

    pieces = out.reshape(GROUP, ROWS, 256)
    attended = [lax.dynamic_index_in_dim(pieces, group, 0, keepdims=False)]
    for r in (1, 2, 3):
        sent = lax.dynamic_index_in_dim(pieces, group ^ r, 0, keepdims=False)
        attended.append(swap(sent, ("xh", "c"), r, 4))
    resid, gated = glu(attended, local, ln_conv_gain[None], weights)

    seq = ("y", "xh", "c")
    below = lax.ppermute(gated[ROWS - HALF :], seq, [(i, i + 1) for i in range(15)])
    above = lax.ppermute(gated[:HALF], seq, [(i + 1, i) for i in range(15)])
    frame = first_frame + jnp.arange(ROWS, dtype=jnp.int32)
    begin, end = spans(frame)
    taps = jnp.stack([begin - frame + HALF, end - frame + HALF], 0)
    blocks = slice(0, None, RB), slice(RB - 1, None, RB)
    plain = jnp.logical_and(
        begin[blocks[1]] <= frame[blocks[0]] - HALF, end[blocks[0]] >= frame[blocks[1]] + HALF
    ).astype(jnp.int32)
    taps = jnp.broadcast_to(taps[:, :, None], (2, ROWS, 128))
    dw = jnp.transpose(dw_kernel.reshape(CONV_K, TILES, 128), (1, 0, 2))
    rest = (taps, dw, ln_mid_gain[None], resid)
    inner = conv_inner(plain, gated, *rest)
    return conv_edges(plain, inner, gated, below, above, *rest)[None]


def solution(mesh):
    fine = Mesh(mesh.devices.reshape(8, 2, 4, 2, 2), ("z", "xl", "y", "xh", "c"))
    dp, seq = ("z", "xl"), ("y", "xh", "c")
    return jax.shard_map(
        body,
        mesh=fine,
        in_specs=(
            P(dp, seq, None),
            P(dp, seq),
            P(),
            P(dp, None),
            P(dp, None),
            P(),
            P(dp, None),
            P(),
            P(),
        ),
        out_specs=P(dp, seq, None),
        check_vma=False,
    )
```

```python
import functools

import jax
import jax.numpy as jnp
from jax import lax
from jax.experimental import pallas as pl
from jax.experimental.pallas import tpu as pltpu
from jax.sharding import Mesh
from jax.sharding import PartitionSpec as P

D = 1536
HEADS = 12
HD = 64
CONV_K = 32
HALF = CONV_K // 2
IDS = 12
WIDTH = HEADS * HD
ROWS = 256
GROUP = 4
CHUNK = GROUP * ROWS
HCOLS = WIDTH // GROUP
LEN = 4096
KB = 512
QT = 512
NEG = -1e30
F32, BF16 = jnp.float32, jnp.bfloat16
ANY = pl.BlockSpec(memory_space=pl.ANY)
VM = pl.BlockSpec(memory_space=pltpu.VMEM)
SM = pl.BlockSpec(memory_space=pltpu.SMEM)


def params(limit_mib):
    return pltpu.CompilerParams(vmem_limit_bytes=limit_mib << 20)


def cost(us):
    return pl.CostEstimate(flops=int(us * 9e8), bytes_accessed=int(us * 2e6), transcendentals=0)


def shift(value, axis, count, step):
    return lax.ppermute(value, axis, [(i, (i + step) % count) for i in range(count)])


def swap(value, axes, mask, count):
    return lax.ppermute(value, axes, [(i, i ^ mask) for i in range(count)])


def along_z(value):
    pairs = []
    for i in range(8):
        pairs += [(2 * i, (i + 1) % 8 * 2), (2 * i + 1, (i + 7) % 8 * 2 + 1)]
    return lax.ppermute(value, ("z", "c"), pairs)


def along_x(value):
    def index(x, c):
        return x % 2 * 4 + x // 2 * 2 + c

    pairs = []
    for x in range(4):
        pairs += [(index(x, 0), index((x + 1) % 4, 0)), (index(x, 1), index((x + 3) % 4, 1))]
    return lax.ppermute(value, ("xl", "xh", "c"), pairs)


def tie(value, other):
    return lax.optimization_barrier((value, other))


def between_cores(value):
    return lax.ppermute(value, "c", [(0, 1), (1, 0)])


def norm(values, gain):
    centre = jnp.mean(values, -1, keepdims=True)
    shifted = values - centre
    spread = jnp.mean(shifted * shifted, -1, keepdims=True)
    return shifted * lax.rsqrt(spread + 1e-05) * gain


def z_owner(z, c, k, own):
    sign = (2 * c - 1) if own else (1 - 2 * c)
    return lax.rem(z + sign * k + 8, 8)


def qkv_kernel(n0, n1, n2, n3, *refs):
    srcs, (kv_ref, q_ref, w, sem) = refs[:8], refs[8:]
    z, xl, c = lax.axis_index("z"), lax.axis_index("xl"), lax.axis_index("c")
    me = lax.axis_index("xh") * 2 + c
    cols = pl.ds(pl.multiple_of(c * 640, 640), 640)
    copies = []
    for i, ref in enumerate(srcs):
        zz = z_owner(z, c, i, True) if i < 5 else z_owner(z, c, i - 4, False)
        for half in range(2):
            owner = zz * 2 + (xl if half == 0 else 1 - xl)
            rows = pl.ds(pl.multiple_of(owner * 96, 96), 96)
            copies.append(
                pltpu.make_async_copy(ref.at[pl.ds(half * 96, 96), cols], w.at[rows], sem)
            )
    for cp in copies:
        cp.start()
    for cp in copies:
        cp.wait()
    for r, ref in enumerate((n0, n1, n2, n3)):
        rows = pl.ds(pl.multiple_of((me ^ r) * ROWS, ROWS), ROWS)
        out = jnp.dot(ref[...], w[...], preferred_element_type=F32).astype(BF16)
        kv_ref[rows, :] = out[:, :384]
        q_ref[rows, :] = out[:, 384:]


def qkv(normed, srcs):
    return pl.pallas_call(
        qkv_kernel,
        name="qkv",
        out_shape=(
            jax.ShapeDtypeStruct((CHUNK, 384), BF16),
            jax.ShapeDtypeStruct((CHUNK, 256), BF16),
        ),
        in_specs=[VM] * 4 + [ANY] * 8,
        out_specs=(VM, VM),
        scratch_shapes=[pltpu.VMEM((D, 640), BF16), pltpu.SemaphoreType.DMA],
        compiler_params=params(12),
        cost_estimate=cost(5),
    )(*normed, *srcs)


def attn_kernel(parts, first, last, scal, q_ref, span, *refs):
    kvs, refs = refs[: len(parts)], refs[len(parts) :]
    if first:
        outs, (qs, vt, m, l, acc) = refs[:-5], refs[-5:]
    else:
        (ml_in, acc_in), outs, (qs, vt, m, l, acc) = refs[:2], refs[2:-5], refs[-5:]
    y = lax.axis_index("y")
    tile = pl.program_id(0)
    offs = [sum(p[2] for p in parts[:i]) // KB for i in range(len(parts))]

    @pl.when(tile == 0)
    def _():
        for kv, off, (_, _, count) in zip(kvs, offs, parts):
            for i in range(count // KB):
                rows = slice(i * KB, (i + 1) * KB)
                vt[off + i, :128] = kv[rows, 256:].T
                vt[off + i, 128:] = kv[rows, 128:256].T[:HD]

    low = lax.broadcasted_iota(jnp.int32, (QT, 128), 1) < HD
    qa, qb = q_ref[:, :128] * BF16(0.125), q_ref[:, 128:] * BF16(0.125)
    zero = jnp.zeros_like(qa)
    qs[0] = jnp.where(low, qa, zero)
    qs[1] = jnp.where(low, zero, qa)
    qs[2] = qb
    if first:
        m[...] = jnp.full_like(m, NEG)
        l[...] = jnp.zeros_like(l)
        acc[...] = jnp.zeros_like(acc)
    else:
        m[...] = ml_in[:8]
        l[...] = ml_in[8:]
        acc[...] = acc_in[...]
    s_first, e_first, s_last, e_last = [scal[tile * 4 + i] for i in range(4)]

    def step(kv, row, block, base, masked):
        if masked:
            frame = lax.broadcasted_iota(jnp.int32, (KB, QT), 0) + base
            keep = jnp.logical_and(frame >= span[0:1, :], frame < span[1:2, :])
        scores = [
            lax.dot_general(
                kv[pl.ds(row, KB), :128] if h < 2 else kv[pl.ds(row, KB), 128:256],
                qs[h],
                (((1,), (1,)), ((), ())),
                preferred_element_type=F32,
            )
            for h in range(3)
        ]
        for h in range(3):
            s = jnp.where(keep, scores[h], NEG) if masked else scores[h]
            old = m[h : h + 1]
            new = jnp.maximum(old, jnp.max(s, axis=0, keepdims=True))
            p = jnp.exp(s - new)
            alpha = jnp.exp(old - new)
            m[h : h + 1] = new
            l[h : h + 1] = alpha * l[h : h + 1] + jnp.sum(p, axis=0, keepdims=True)
            rows = slice(h * HD, (h + 1) * HD)
            pv = jnp.dot(vt[block, rows], p.astype(BF16), preferred_element_type=F32)
            acc[rows] = alpha * acc[rows] + pv

    for kv, block, (off, start, count) in zip(kvs, offs, parts):
        begin = lax.rem(y + off + 4, 4) * CHUNK + start
        low_i = jnp.clip(lax.div(jnp.maximum(s_first - begin, 0), KB), 0, count // KB)
        high_i = jnp.clip(lax.div(jnp.maximum(e_last - begin, 0) + KB - 1, KB), 0, count // KB)

        @pl.loop(low_i, high_i)
        def _(i):
            base = begin + i * KB
            row = pl.multiple_of(i * KB, KB)
            plain = jnp.logical_and(s_last <= base, e_first >= base + KB)

            @pl.when(plain)
            def _():
                step(kv, row, block + i, base, False)

            @pl.when(jnp.logical_not(plain))
            def _():
                step(kv, row, block + i, base, True)

    if last:
        (out,) = outs
        for h in range(3):
            rows = slice(h * HD, (h + 1) * HD)
            acc[rows] = acc[rows] / l[h : h + 1]
        out[:, :128] = acc[:128].T.astype(BF16)
        tail = jnp.concatenate([acc[128:], jnp.zeros((HD, QT), F32)], 0)
        out[:, 128:] = tail.T.astype(BF16)
    else:
        ml_out, acc_out = outs
        ml_out[:8] = m[...]
        ml_out[8:] = l[...]
        acc_out[...] = acc[...]


def attend(parts, q, span, scal, kvs, state, last, us):
    first = state is None

    def rows(count):
        return pl.BlockSpec((QT, count), lambda i: (i, 0))

    def cols(count):
        return pl.BlockSpec((count, QT), lambda i: (0, i))

    state_shapes = (
        jax.ShapeDtypeStruct((16, CHUNK), F32),
        jax.ShapeDtypeStruct((HCOLS, CHUNK), F32),
    )
    return pl.pallas_call(
        functools.partial(attn_kernel, parts, first, last),
        name="attend",
        grid=(CHUNK // QT,),
        out_shape=jax.ShapeDtypeStruct((CHUNK, 256), BF16) if last else state_shapes,
        in_specs=[SM, rows(256), cols(8)]
        + [VM] * len(kvs)
        + ([] if first else [cols(16), cols(HCOLS)]),
        out_specs=rows(256) if last else (cols(16), cols(HCOLS)),
        scratch_shapes=[
            pltpu.VMEM((3, QT, 128), BF16),
            pltpu.VMEM((sum(p[2] for p in parts) // KB, HCOLS, KB), BF16),
            pltpu.VMEM((8, QT), F32),
            pltpu.VMEM((8, QT), F32),
            pltpu.VMEM((HCOLS, QT), F32),
        ],
        compiler_params=params(18),
        cost_estimate=cost(us),
    )(scal, q, span, *kvs, *(() if first else state))


def glu_kernel(a0, a1, a2, a3, local, gain, *refs):
    srcs, (resid_ref, gated_ref, wo, wv, wg, sem_o, sem_g) = refs[:16], refs[16:]
    z, xl, c = lax.axis_index("z"), lax.axis_index("xl"), lax.axis_index("c")
    me = lax.axis_index("xh") * 2 + c
    out_copies, glu_copies = [], []

    def rows(owner, count):
        return pl.ds(pl.multiple_of(owner * count, count), count)

    for half in range(2):
        for i in range(8):
            ref = srcs[8 * half + i]
            zz = z_owner(z, c, i, True) if i < 5 else z_owner(z, c, i - 4, False)
            owner = zz * 2 + (xl if half == 0 else 1 - xl)
            out_copies.append(
                pltpu.make_async_copy(ref.at[pl.ds(0, 48)], wo.at[rows(owner, 48)], sem_o)
            )
            glu_copies.append(
                pltpu.make_async_copy(ref.at[pl.ds(48, 96)], wv.at[rows(owner, 96)], sem_g)
            )
            glu_copies.append(
                pltpu.make_async_copy(ref.at[pl.ds(144, 96)], wg.at[rows(owner, 96)], sem_g)
            )
    for cp in out_copies + glu_copies:
        cp.start()
    for cp in out_copies:
        cp.wait()
    attn = jnp.zeros((ROWS, D), F32)
    for r, ref in enumerate((a0, a1, a2, a3)):
        part = wo[rows(me ^ r, HCOLS), :]
        attn = attn + jnp.dot(ref[:, :HCOLS], part, preferred_element_type=F32)
    resid = (local[...].astype(F32) + attn).astype(BF16)
    resid_ref[...] = resid
    glu_in = norm(resid.astype(F32), gain[...]).astype(BF16)
    for cp in glu_copies:
        cp.wait()
    for j in range(0, D, 512):
        value = jnp.dot(glu_in, wv[:, j : j + 512], preferred_element_type=F32)
        gate = jnp.dot(glu_in, wg[:, j : j + 512], preferred_element_type=F32)
        gated_ref[:, j : j + 512] = (value * jax.nn.sigmoid(gate)).astype(BF16)


def glu(attended, local, gain, srcs):
    return pl.pallas_call(
        glu_kernel,
        name="glu",
        out_shape=(jax.ShapeDtypeStruct((ROWS, D), BF16),) * 2,
        in_specs=[VM] * 6 + [ANY] * 16,
        out_specs=(VM, VM),
        scratch_shapes=[
            pltpu.VMEM((WIDTH, D), BF16),
            pltpu.VMEM((D, D), BF16),
            pltpu.VMEM((D, D), BF16),
            pltpu.SemaphoreType.DMA,
            pltpu.SemaphoreType.DMA,
        ],
        compiler_params=params(26),
        cost_estimate=cost(10),
    )(*attended, local, gain, *srcs)


RB = 32
CT = 4
TILES = D // 128


def conv_block(i, scal, taps, dw, xb, cv, x0, c0):
    r0 = pl.multiple_of(i * RB, RB)

    def block(group, masked):
        total = [jnp.zeros((RB, 128), F32) for _ in range(CT)]
        if masked:
            begin, end = taps[0, pl.ds(r0, RB), :], taps[1, pl.ds(r0, RB), :]
        for j in range(CONV_K):
            if masked:
                keep = jnp.logical_and(begin <= j, j < end)
            for t in range(CT):
                tile = group * CT + t
                term = xb[tile, pl.ds(x0 + j, RB), :] * dw[tile, j : j + 1, :]
                total[t] = total[t] + (jnp.where(keep, term, 0.0) if masked else term)
        for t in range(CT):
            cv[group * CT + t, pl.ds(c0, RB), :] = total[t]

    @pl.loop(0, TILES // CT)
    def _(group):
        @pl.when(scal[i] == 1)
        def _():
            block(group, False)

        @pl.when(scal[i] == 0)
        def _():
            block(group, True)


def finish(cv, cv_rows, gain, resid, resid_rows, out, out_rows):
    parts = [cv[t, cv_rows, :] for t in range(TILES)]
    centre = jnp.sum(sum(parts), -1, keepdims=True) * (1.0 / D)
    parts = [p - centre for p in parts]
    spread = jnp.sum(sum(p * p for p in parts), -1, keepdims=True) * (1.0 / D)
    scale = lax.rsqrt(spread + 1e-05)
    for t in range(TILES):
        cols = slice(t * 128, (t + 1) * 128)
        mid = parts[t] * scale * gain[:, cols]
        res = resid[resid_rows, cols].astype(F32)
        out[out_rows, cols] = (res + mid * jax.nn.sigmoid(mid)).astype(BF16)


def inner_kernel(scal, gated, taps, dw, gain, resid, out, xb, cv):
    for t in range(TILES):
        xb[t] = gated[:, t * 128 : (t + 1) * 128].astype(F32)

    @pl.loop(1, ROWS // RB - 1)
    def _(i):
        r0 = pl.multiple_of(i * RB, RB)
        conv_block(i, scal, taps, dw, xb, cv, r0 - HALF, r0)

    @pl.loop(0, (ROWS - 2 * RB) // 64)
    def _(i):
        rows = pl.ds(pl.multiple_of(RB + i * 64, RB), 64)
        finish(cv, rows, gain, resid, rows, out, rows)


def edge_kernel(scal, _, gated, below, above, taps, dw, gain, resid, out, xb, cv):
    part = pl.program_id(0)
    near = RB + HALF

    @pl.when(part == 0)
    def _():
        for t in range(TILES):
            cols = slice(t * 128, (t + 1) * 128)
            xb[t, :HALF] = below[:, cols].astype(F32)
            xb[t, HALF:] = gated[:near, cols].astype(F32)

    @pl.when(part == 1)
    def _():
        for t in range(TILES):
            cols = slice(t * 128, (t + 1) * 128)
            xb[t, :near] = gated[ROWS - near :, cols].astype(F32)
            xb[t, near:] = above[:, cols].astype(F32)

    block = part * (ROWS // RB - 1)
    conv_block(block, scal, taps, dw, xb, cv, 0, 0)
    rows = slice(0, RB)
    finish(cv, rows, gain, resid, pl.ds(pl.multiple_of(block * RB, RB), RB), out, rows)


def conv_inner(scal, gated, taps, dw, gain, resid):
    return pl.pallas_call(
        inner_kernel,
        name="inner",
        out_shape=jax.ShapeDtypeStruct((ROWS, D), BF16),
        in_specs=[SM] + [VM] * 5,
        out_specs=VM,
        scratch_shapes=[
            pltpu.VMEM((TILES, ROWS, 128), F32),
            pltpu.VMEM((TILES, ROWS, 128), F32),
        ],
        compiler_params=params(14),
        cost_estimate=cost(8),
    )(scal, gated, taps, dw, gain, resid)


def conv_edges(scal, inner, gated, below, above, taps, dw, gain, resid):
    return pl.pallas_call(
        edge_kernel,
        name="edges",
        grid=(2,),
        out_shape=jax.ShapeDtypeStruct((ROWS, D), BF16),
        in_specs=[SM, ANY] + [VM] * 7,
        out_specs=pl.BlockSpec((RB, D), lambda i: (i * (ROWS // RB - 1), 0)),
        scratch_shapes=[
            pltpu.VMEM((TILES, RB + CONV_K, 128), F32),
            pltpu.VMEM((TILES, RB, 128), F32),
        ],
        input_output_aliases={1: 0},
        compiler_params=params(14),
        cost_estimate=cost(3),
    )(scal, inner, gated, below, above, taps, dw, gain, resid)


def body(
    frames, segment_ids, ln_attn_gain, w_qkv, w_out, ln_conv_gain, w_glu, dw_kernel, ln_mid_gain
):
    local = frames[0]
    y, xh, c = lax.axis_index("y"), lax.axis_index("xh"), lax.axis_index("c")
    group = xh * 2 + c
    first_frame = (y * GROUP + group) * ROWS

    wq, wk, wv = [
        lax.dynamic_slice_in_dim(w_qkv, part * WIDTH + xh * 2 * HCOLS, 2 * HCOLS, 1)
        for part in range(3)
    ]
    columns = []
    for j in (0, HCOLS):
        columns += [wk[:, j : j + 128], wv[:, j + 128 : j + HCOLS], wk[:, j + 128 : j + HCOLS]]
        columns += [wv[:, j : j + 128], wq[:, j : j + 128], jnp.zeros((96, HD), BF16)]
        columns += [wq[:, j + 128 : j + HCOLS]]
    own = jnp.concatenate(columns, axis=1)
    ids = lax.broadcasted_iota(jnp.int32, (IDS, ROWS), 0)
    counts = jnp.sum((segment_ids == ids).astype(jnp.int32), axis=1)[None]
    hops = (("c", 1, 2), ("xh", 1, 2), ("y", 1, 4), ("y", 2, 4))
    ring = [jnp.concatenate([own, swap(own, "xl", 1, 2)], axis=0)]
    for step_hops in (hops[:1], hops[1:2], hops[2:], ()):
        src = ring[-1]
        for axis, mask, count in step_hops:
            counts = counts + swap(counts, axis, mask, count)
        if step_hops:
            src, counts = tie(src, counts)
        ring.append(along_z(src))
    srcs = ring + [between_cores(v) for v in ring[1:4]]

    normed = norm(local.astype(F32), ln_attn_gain).astype(BF16)
    n2, srcs[3] = tie(swap(normed, "xh", 1, 2), ring[3])
    pieces = [normed, between_cores(normed), n2, between_cores(n2)]
    kv, q = qkv(pieces, srcs)

    ends = jnp.cumsum(counts[0])
    starts = ends - counts[0]

    def spans(frame):
        begin = jnp.max(jnp.where(starts[:, None] <= frame[None], starts[:, None], 0), 0)
        end = jnp.min(jnp.where(ends[:, None] > frame[None], ends[:, None], LEN), 0)
        return begin, end

    begin, end = spans(y * CHUNK + jnp.arange(CHUNK, dtype=jnp.int32))
    span = jnp.concatenate([begin[None], end[None], jnp.zeros((6, CHUNK), jnp.int32)], 0)
    firsts, lasts = slice(0, None, QT), slice(QT - 1, None, QT)
    scal = jnp.stack([begin[firsts], end[firsts], begin[lasts], end[lasts]], 1).reshape(-1)

    both = jnp.concatenate([w_out, w_glu[:, :D], w_glu[:, D:]], axis=0)
    late = ring[3][0, 0].astype(F32)
    w0 = jnp.where(late == jnp.inf, jnp.zeros_like(both), both)
    w1 = along_z(w0)
    src, kv_later = tie(w1, kv)
    w2 = along_z(src)
    x0, x1, x2 = along_x(w0), along_x(w1), along_x(w2)
    up, down = shift(kv, "y", 4, 1), shift(kv, "y", 4, -1)
    common = (q, span, scal)
    kv, w1_later = tie(kv_later, w1)
    state = attend(((0, 0, 1024),), *common, (kv,), None, False, 7)
    src, mark = tie(w2, state[0])
    w3 = along_z(src)
    w4 = along_z(w3)
    far_src, mark = tie((up[:512], down[512:]), mark)
    far0, far1 = shift(far_src[0], "y", 4, 1), shift(far_src[1], "y", 4, -1)
    x3, x4 = along_x(w3), along_x(w4)
    up, w2_later, x0 = lax.optimization_barrier((up, w2, x0))
    down, w3_later, x1 = lax.optimization_barrier((down, w3, x1))
    far0, w4_later = tie(far0, w4)
    z_set = [w0, w1_later, w2_later, w3_later, w4_later]
    state = attend(((-1, 0, 1024),), *common, (up,), (mark, state[1]), False, 10)
    state = attend(((1, 0, 1024),), *common, (down,), state, False, 14)
    mark, x2 = tie(state[0], x2)
    state = (mark, state[1])
    x_set = [x0, x1, x2, x3, x4]
    weights = []
    for values in (z_set, x_set):
        weights += values + [between_cores(v) for v in values[1:4]]
    out = attend(((-2, 0, 512), (2, 512, 512)), *common, (far0, far1), state, True, 7)

    pieces = out.reshape(GROUP, ROWS, 256)
    attended = [lax.dynamic_index_in_dim(pieces, group, 0, keepdims=False)]
    for r in (1, 2, 3):
        sent = lax.dynamic_index_in_dim(pieces, group ^ r, 0, keepdims=False)
        attended.append(swap(sent, ("xh", "c"), r, 4))
    resid, gated = glu(attended, local, ln_conv_gain[None], weights)

    seq = ("y", "xh", "c")
    below = lax.ppermute(gated[ROWS - HALF :], seq, [(i, i + 1) for i in range(15)])
    above = lax.ppermute(gated[:HALF], seq, [(i + 1, i) for i in range(15)])
    frame = first_frame + jnp.arange(ROWS, dtype=jnp.int32)
    begin, end = spans(frame)
    taps = jnp.stack([begin - frame + HALF, end - frame + HALF], 0)
    blocks = slice(0, None, RB), slice(RB - 1, None, RB)
    plain = jnp.logical_and(
        begin[blocks[1]] <= frame[blocks[0]] - HALF, end[blocks[0]] >= frame[blocks[1]] + HALF
    ).astype(jnp.int32)
    taps = jnp.broadcast_to(taps[:, :, None], (2, ROWS, 128))
    dw = jnp.transpose(dw_kernel.reshape(CONV_K, TILES, 128), (1, 0, 2))
    rest = (taps, dw, ln_mid_gain[None], resid)
    inner = conv_inner(plain, gated, *rest)
    return conv_edges(plain, inner, gated, below, above, *rest)[None]


def solution(mesh):
    fine = Mesh(mesh.devices.reshape(8, 2, 4, 2, 2), ("z", "xl", "y", "xh", "c"))
    dp, seq = ("z", "xl"), ("y", "xh", "c")
    return jax.shard_map(
        body,
        mesh=fine,
        in_specs=(
            P(dp, seq, None),
            P(dp, seq),
            P(),
            P(dp, None),
            P(dp, None),
            P(),
            P(dp, None),
            P(),
            P(),
        ),
        out_specs=P(dp, seq, None),
        check_vma=False,
    )
```

```python
import functools

import jax
import jax.numpy as jnp
from jax import lax
from jax.experimental import pallas as pl
from jax.experimental.pallas import tpu as pltpu
from jax.sharding import Mesh
from jax.sharding import PartitionSpec as P

D = 1536
HEADS = 12
HD = 64
CONV_K = 32
HALF = CONV_K // 2
IDS = 12
WIDTH = HEADS * HD
ROWS = 256
GROUP = 4
CHUNK = GROUP * ROWS
HCOLS = WIDTH // GROUP
LEN = 4096
KB = 512
QT = 512
NEG = -1e30
F32, BF16 = jnp.float32, jnp.bfloat16
ANY = pl.BlockSpec(memory_space=pl.ANY)
VM = pl.BlockSpec(memory_space=pltpu.VMEM)
SM = pl.BlockSpec(memory_space=pltpu.SMEM)


def params(limit_mib):
    return pltpu.CompilerParams(vmem_limit_bytes=limit_mib << 20)


def cost(us):
    return pl.CostEstimate(flops=int(us * 9e8), bytes_accessed=int(us * 2e6), transcendentals=0)


def shift(value, axis, count, step):
    return lax.ppermute(value, axis, [(i, (i + step) % count) for i in range(count)])


def swap(value, axes, mask, count):
    return lax.ppermute(value, axes, [(i, i ^ mask) for i in range(count)])


def along_z(value):
    pairs = []
    for i in range(8):
        pairs += [(2 * i, (i + 1) % 8 * 2), (2 * i + 1, (i + 7) % 8 * 2 + 1)]
    return lax.ppermute(value, ("z", "c"), pairs)


def along_x(value):
    def index(x, c):
        return x % 2 * 4 + x // 2 * 2 + c

    pairs = []
    for x in range(4):
        pairs += [(index(x, 0), index((x + 1) % 4, 0)), (index(x, 1), index((x + 3) % 4, 1))]
    return lax.ppermute(value, ("xl", "xh", "c"), pairs)


def tie(value, other):
    return lax.optimization_barrier((value, other))


def between_cores(value):
    return lax.ppermute(value, "c", [(0, 1), (1, 0)])


def norm(values, gain):
    centre = jnp.mean(values, -1, keepdims=True)
    shifted = values - centre
    spread = jnp.mean(shifted * shifted, -1, keepdims=True)
    return shifted * lax.rsqrt(spread + 1e-05) * gain


def z_owner(z, c, k, own):
    sign = (2 * c - 1) if own else (1 - 2 * c)
    return lax.rem(z + sign * k + 8, 8)


def qkv_kernel(n0, n1, n2, n3, *refs):
    srcs, (kv_ref, q_ref, w, sem) = refs[:8], refs[8:]
    z, xl, c = lax.axis_index("z"), lax.axis_index("xl"), lax.axis_index("c")
    me = lax.axis_index("xh") * 2 + c
    cols = pl.ds(pl.multiple_of(c * 640, 640), 640)
    copies = []
    for i, ref in enumerate(srcs):
        zz = z_owner(z, c, i, True) if i < 5 else z_owner(z, c, i - 4, False)
        for half in range(2):
            owner = zz * 2 + (xl if half == 0 else 1 - xl)
            rows = pl.ds(pl.multiple_of(owner * 96, 96), 96)
            copies.append(
                pltpu.make_async_copy(ref.at[pl.ds(half * 96, 96), cols], w.at[rows], sem)
            )
    for cp in copies:
        cp.start()
    for cp in copies:
        cp.wait()
    for r, ref in enumerate((n0, n1, n2, n3)):
        rows = pl.ds(pl.multiple_of((me ^ r) * ROWS, ROWS), ROWS)
        out = jnp.dot(ref[...], w[...], preferred_element_type=F32).astype(BF16)
        kv_ref[rows, :] = out[:, :384]
        q_ref[rows, :] = out[:, 384:]


def qkv(normed, srcs):
    return pl.pallas_call(
        qkv_kernel,
        name="qkv",
        out_shape=(
            jax.ShapeDtypeStruct((CHUNK, 384), BF16),
            jax.ShapeDtypeStruct((CHUNK, 256), BF16),
        ),
        in_specs=[VM] * 4 + [ANY] * 8,
        out_specs=(VM, VM),
        scratch_shapes=[pltpu.VMEM((D, 640), BF16), pltpu.SemaphoreType.DMA],
        compiler_params=params(12),
        cost_estimate=cost(5),
    )(*normed, *srcs)


def attn_kernel(parts, first, last, scal, q_ref, span, *refs):
    kvs, refs = refs[: len(parts)], refs[len(parts) :]
    if first:
        outs, (qs, vt, m, l, acc) = refs[:-5], refs[-5:]
    else:
        (ml_in, acc_in), outs, (qs, vt, m, l, acc) = refs[:2], refs[2:-5], refs[-5:]
    y = lax.axis_index("y")
    tile = pl.program_id(0)
    offs = [sum(p[2] for p in parts[:i]) // KB for i in range(len(parts))]

    @pl.when(tile == 0)
    def _():
        for kv, off, (_, _, count) in zip(kvs, offs, parts):
            for i in range(count // KB):
                rows = slice(i * KB, (i + 1) * KB)
                vt[off + i, :128] = kv[rows, 256:].T
                vt[off + i, 128:] = kv[rows, 128:256].T[:HD]

    low = lax.broadcasted_iota(jnp.int32, (QT, 128), 1) < HD
    qa, qb = q_ref[:, :128] * BF16(0.125), q_ref[:, 128:] * BF16(0.125)
    zero = jnp.zeros_like(qa)
    qs[0] = jnp.where(low, qa, zero)
    qs[1] = jnp.where(low, zero, qa)
    qs[2] = qb
    if first:
        m[...] = jnp.full_like(m, NEG)
        l[...] = jnp.zeros_like(l)
        acc[...] = jnp.zeros_like(acc)
    else:
        m[...] = ml_in[:8]
        l[...] = ml_in[8:]
        acc[...] = acc_in[...]
    s_first, e_first, s_last, e_last = [scal[tile * 4 + i] for i in range(4)]

    def step(kv, row, block, base, masked):
        if masked:
            frame = lax.broadcasted_iota(jnp.int32, (KB, QT), 0) + base
            keep = jnp.logical_and(frame >= span[0:1, :], frame < span[1:2, :])
        scores = [
            lax.dot_general(
                kv[pl.ds(row, KB), :128] if h < 2 else kv[pl.ds(row, KB), 128:256],
                qs[h],
                (((1,), (1,)), ((), ())),
                preferred_element_type=F32,
            )
            for h in range(3)
        ]
        for h in range(3):
            s = jnp.where(keep, scores[h], NEG) if masked else scores[h]
            old = m[h : h + 1]
            new = jnp.maximum(old, jnp.max(s, axis=0, keepdims=True))
            p = jnp.exp(s - new)
            alpha = jnp.exp(old - new)
            m[h : h + 1] = new
            l[h : h + 1] = alpha * l[h : h + 1] + jnp.sum(p, axis=0, keepdims=True)
            rows = slice(h * HD, (h + 1) * HD)
            pv = jnp.dot(vt[block, rows], p.astype(BF16), preferred_element_type=F32)
            acc[rows] = alpha * acc[rows] + pv

    for kv, block, (off, start, count) in zip(kvs, offs, parts):
        begin = lax.rem(y + off + 4, 4) * CHUNK + start
        low_i = jnp.clip(lax.div(jnp.maximum(s_first - begin, 0), KB), 0, count // KB)
        high_i = jnp.clip(lax.div(jnp.maximum(e_last - begin, 0) + KB - 1, KB), 0, count // KB)

        @pl.loop(low_i, high_i)
        def _(i):
            base = begin + i * KB
            row = pl.multiple_of(i * KB, KB)
            plain = jnp.logical_and(s_last <= base, e_first >= base + KB)

            @pl.when(plain)
            def _():
                step(kv, row, block + i, base, False)

            @pl.when(jnp.logical_not(plain))
            def _():
                step(kv, row, block + i, base, True)

    if last:
        (out,) = outs
        for h in range(3):
            rows = slice(h * HD, (h + 1) * HD)
            acc[rows] = acc[rows] / l[h : h + 1]
        out[:, :128] = acc[:128].T.astype(BF16)
        tail = jnp.concatenate([acc[128:], jnp.zeros((HD, QT), F32)], 0)
        out[:, 128:] = tail.T.astype(BF16)
    else:
        ml_out, acc_out = outs
        ml_out[:8] = m[...]
        ml_out[8:] = l[...]
        acc_out[...] = acc[...]


def attend(parts, q, span, scal, kvs, state, last, us):
    first = state is None

    def rows(count):
        return pl.BlockSpec((QT, count), lambda i: (i, 0))

    def cols(count):
        return pl.BlockSpec((count, QT), lambda i: (0, i))

    state_shapes = (
        jax.ShapeDtypeStruct((16, CHUNK), F32),
        jax.ShapeDtypeStruct((HCOLS, CHUNK), F32),
    )
    return pl.pallas_call(
        functools.partial(attn_kernel, parts, first, last),
        name="attend",
        grid=(CHUNK // QT,),
        out_shape=jax.ShapeDtypeStruct((CHUNK, 256), BF16) if last else state_shapes,
        in_specs=[SM, rows(256), cols(8)]
        + [VM] * len(kvs)
        + ([] if first else [cols(16), cols(HCOLS)]),
        out_specs=rows(256) if last else (cols(16), cols(HCOLS)),
        scratch_shapes=[
            pltpu.VMEM((3, QT, 128), BF16),
            pltpu.VMEM((sum(p[2] for p in parts) // KB, HCOLS, KB), BF16),
            pltpu.VMEM((8, QT), F32),
            pltpu.VMEM((8, QT), F32),
            pltpu.VMEM((HCOLS, QT), F32),
        ],
        compiler_params=params(18),
        cost_estimate=cost(us),
    )(scal, q, span, *kvs, *(() if first else state))


def glu_kernel(a0, a1, a2, a3, local, gain, *refs):
    srcs, (resid_ref, gated_ref, wo, wv, wg, sem_o, sem_g) = refs[:16], refs[16:]
    z, xl, c = lax.axis_index("z"), lax.axis_index("xl"), lax.axis_index("c")
    me = lax.axis_index("xh") * 2 + c
    out_copies, glu_copies = [], []

    def rows(owner, count):
        return pl.ds(pl.multiple_of(owner * count, count), count)

    for half in range(2):
        for i in range(8):
            ref = srcs[8 * half + i]
            zz = z_owner(z, c, i, True) if i < 5 else z_owner(z, c, i - 4, False)
            owner = zz * 2 + (xl if half == 0 else 1 - xl)
            out_copies.append(
                pltpu.make_async_copy(ref.at[pl.ds(0, 48)], wo.at[rows(owner, 48)], sem_o)
            )
            glu_copies.append(
                pltpu.make_async_copy(ref.at[pl.ds(48, 96)], wv.at[rows(owner, 96)], sem_g)
            )
            glu_copies.append(
                pltpu.make_async_copy(ref.at[pl.ds(144, 96)], wg.at[rows(owner, 96)], sem_g)
            )
    for cp in out_copies + glu_copies:
        cp.start()
    for cp in out_copies:
        cp.wait()
    attn = jnp.zeros((ROWS, D), F32)
    for r, ref in enumerate((a0, a1, a2, a3)):
        part = wo[rows(me ^ r, HCOLS), :]
        attn = attn + jnp.dot(ref[:, :HCOLS], part, preferred_element_type=F32)
    resid = (local[...].astype(F32) + attn).astype(BF16)
    resid_ref[...] = resid
    glu_in = norm(resid.astype(F32), gain[...]).astype(BF16)
    for cp in glu_copies:
        cp.wait()
    for j in range(0, D, 512):
        value = jnp.dot(glu_in, wv[:, j : j + 512], preferred_element_type=F32)
        gate = jnp.dot(glu_in, wg[:, j : j + 512], preferred_element_type=F32)
        gated_ref[:, j : j + 512] = (value * jax.nn.sigmoid(gate)).astype(BF16)


def glu(attended, local, gain, srcs):
    return pl.pallas_call(
        glu_kernel,
        name="glu",
        out_shape=(jax.ShapeDtypeStruct((ROWS, D), BF16),) * 2,
        in_specs=[VM] * 6 + [ANY] * 16,
        out_specs=(VM, VM),
        scratch_shapes=[
            pltpu.VMEM((WIDTH, D), BF16),
            pltpu.VMEM((D, D), BF16),
            pltpu.VMEM((D, D), BF16),
            pltpu.SemaphoreType.DMA,
            pltpu.SemaphoreType.DMA,
        ],
        compiler_params=params(26),
        cost_estimate=cost(10),
    )(*attended, local, gain, *srcs)


RB = 32
CT = 4
TILES = D // 128


def conv_block(i, scal, taps, dw, xb, cv, x0, c0):
    r0 = pl.multiple_of(i * RB, RB)

    def block(group, masked):
        total = [jnp.zeros((RB, 128), F32) for _ in range(CT)]
        if masked:
            begin, end = taps[0, pl.ds(r0, RB), :], taps[1, pl.ds(r0, RB), :]
        for j in range(CONV_K):
            if masked:
                keep = begin <= j if j <= HALF else j < end
            for t in range(CT):
                tile = group * CT + t
                term = xb[tile, pl.ds(x0 + j, RB), :] * dw[tile, j : j + 1, :]
                total[t] = total[t] + (jnp.where(keep, term, 0.0) if masked else term)
        for t in range(CT):
            cv[group * CT + t, pl.ds(c0, RB), :] = total[t]

    @pl.loop(0, TILES // CT)
    def _(group):
        @pl.when(scal[i] == 1)
        def _():
            block(group, False)

        @pl.when(scal[i] == 0)
        def _():
            block(group, True)


def finish(cv, cv_rows, gain, resid, resid_rows, out, out_rows):
    parts = [cv[t, cv_rows, :] for t in range(TILES)]
    centre = jnp.sum(sum(parts), -1, keepdims=True) * (1.0 / D)
    parts = [p - centre for p in parts]
    spread = jnp.sum(sum(p * p for p in parts), -1, keepdims=True) * (1.0 / D)
    scale = lax.rsqrt(spread + 1e-05)
    for t in range(TILES):
        cols = slice(t * 128, (t + 1) * 128)
        mid = parts[t] * scale * gain[:, cols]
        res = resid[resid_rows, cols].astype(F32)
        out[out_rows, cols] = (res + mid * jax.nn.sigmoid(mid)).astype(BF16)


def inner_kernel(scal, gated, taps, dw, gain, resid, out, xb, cv):
    for t in range(TILES):
        xb[t] = gated[:, t * 128 : (t + 1) * 128].astype(F32)

    @pl.loop(1, ROWS // RB - 1)
    def _(i):
        r0 = pl.multiple_of(i * RB, RB)
        conv_block(i, scal, taps, dw, xb, cv, r0 - HALF, r0)

    @pl.loop(0, (ROWS - 2 * RB) // 64)
    def _(i):
        rows = pl.ds(pl.multiple_of(RB + i * 64, RB), 64)
        finish(cv, rows, gain, resid, rows, out, rows)


def edge_kernel(scal, _, gated, below, above, taps, dw, gain, resid, out, xb, cv):
    part = pl.program_id(0)
    near = RB + HALF

    @pl.when(part == 0)
    def _():
        for t in range(TILES):
            cols = slice(t * 128, (t + 1) * 128)
            xb[t, :HALF] = below[:, cols].astype(F32)
            xb[t, HALF:] = gated[:near, cols].astype(F32)

    @pl.when(part == 1)
    def _():
        for t in range(TILES):
            cols = slice(t * 128, (t + 1) * 128)
            xb[t, :near] = gated[ROWS - near :, cols].astype(F32)
            xb[t, near:] = above[:, cols].astype(F32)

    block = part * (ROWS // RB - 1)
    conv_block(block, scal, taps, dw, xb, cv, 0, 0)
    rows = slice(0, RB)
    finish(cv, rows, gain, resid, pl.ds(pl.multiple_of(block * RB, RB), RB), out, rows)


def conv_inner(scal, gated, taps, dw, gain, resid):
    return pl.pallas_call(
        inner_kernel,
        name="inner",
        out_shape=jax.ShapeDtypeStruct((ROWS, D), BF16),
        in_specs=[SM] + [VM] * 5,
        out_specs=VM,
        scratch_shapes=[
            pltpu.VMEM((TILES, ROWS, 128), F32),
            pltpu.VMEM((TILES, ROWS, 128), F32),
        ],
        compiler_params=params(14),
        cost_estimate=cost(8),
    )(scal, gated, taps, dw, gain, resid)


def conv_edges(scal, inner, gated, below, above, taps, dw, gain, resid):
    return pl.pallas_call(
        edge_kernel,
        name="edges",
        grid=(2,),
        out_shape=jax.ShapeDtypeStruct((ROWS, D), BF16),
        in_specs=[SM, ANY] + [VM] * 7,
        out_specs=pl.BlockSpec((RB, D), lambda i: (i * (ROWS // RB - 1), 0)),
        scratch_shapes=[
            pltpu.VMEM((TILES, RB + CONV_K, 128), F32),
            pltpu.VMEM((TILES, RB, 128), F32),
        ],
        input_output_aliases={1: 0},
        compiler_params=params(14),
        cost_estimate=cost(3),
    )(scal, inner, gated, below, above, taps, dw, gain, resid)


def body(
    frames, segment_ids, ln_attn_gain, w_qkv, w_out, ln_conv_gain, w_glu, dw_kernel, ln_mid_gain
):
    local = frames[0]
    y, xh, c = lax.axis_index("y"), lax.axis_index("xh"), lax.axis_index("c")
    group = xh * 2 + c
    first_frame = (y * GROUP + group) * ROWS

    wq, wk, wv = [
        lax.dynamic_slice_in_dim(w_qkv, part * WIDTH + xh * 2 * HCOLS, 2 * HCOLS, 1)
        for part in range(3)
    ]
    columns = []
    for j in (0, HCOLS):
        columns += [wk[:, j : j + 128], wv[:, j + 128 : j + HCOLS], wk[:, j + 128 : j + HCOLS]]
        columns += [wv[:, j : j + 128], wq[:, j : j + 128], jnp.zeros((96, HD), BF16)]
        columns += [wq[:, j + 128 : j + HCOLS]]
    own = jnp.concatenate(columns, axis=1)
    ids = lax.broadcasted_iota(jnp.int32, (IDS, ROWS), 0)
    counts = jnp.sum((segment_ids == ids).astype(jnp.int32), axis=1)[None]
    hops = (("c", 1, 2), ("xh", 1, 2), ("y", 1, 4), ("y", 2, 4))
    ring = [jnp.concatenate([own, swap(own, "xl", 1, 2)], axis=0)]
    for step_hops in (hops[:1], hops[1:2], hops[2:], ()):
        src = ring[-1]
        for axis, mask, count in step_hops:
            counts = counts + swap(counts, axis, mask, count)
        if step_hops:
            src, counts = tie(src, counts)
        ring.append(along_z(src))
    srcs = ring + [between_cores(v) for v in ring[1:4]]

    normed = norm(local.astype(F32), ln_attn_gain).astype(BF16)
    n2, srcs[3] = tie(swap(normed, "xh", 1, 2), ring[3])
    pieces = [normed, between_cores(normed), n2, between_cores(n2)]
    kv, q = qkv(pieces, srcs)

    ends = jnp.cumsum(counts[0])
    starts = ends - counts[0]

    def spans(frame):
        begin = jnp.max(jnp.where(starts[:, None] <= frame[None], starts[:, None], 0), 0)
        end = jnp.min(jnp.where(ends[:, None] > frame[None], ends[:, None], LEN), 0)
        return begin, end

    begin, end = spans(y * CHUNK + jnp.arange(CHUNK, dtype=jnp.int32))
    span = jnp.concatenate([begin[None], end[None], jnp.zeros((6, CHUNK), jnp.int32)], 0)
    firsts, lasts = slice(0, None, QT), slice(QT - 1, None, QT)
    scal = jnp.stack([begin[firsts], end[firsts], begin[lasts], end[lasts]], 1).reshape(-1)

    both = jnp.concatenate([w_out, w_glu[:, :D], w_glu[:, D:]], axis=0)
    late = ring[3][0, 0].astype(F32)
    w0 = jnp.where(late == jnp.inf, jnp.zeros_like(both), both)
    w1 = along_z(w0)
    src, kv_later = tie(w1, kv)
    w2 = along_z(src)
    x0, x1, x2 = along_x(w0), along_x(w1), along_x(w2)
    up, down = shift(kv, "y", 4, 1), shift(kv, "y", 4, -1)
    common = (q, span, scal)
    kv, w1_later = tie(kv_later, w1)
    state = attend(((0, 0, 1024),), *common, (kv,), None, False, 7)
    src, mark = tie(w2, state[0])
    w3 = along_z(src)
    w4 = along_z(w3)
    far_src, mark = tie((up[:512], down[512:]), mark)
    far0, far1 = shift(far_src[0], "y", 4, 1), shift(far_src[1], "y", 4, -1)
    x3, x4 = along_x(w3), along_x(w4)
    up, w2_later, x0 = lax.optimization_barrier((up, w2, x0))
    down, w3_later, x1 = lax.optimization_barrier((down, w3, x1))
    far0, w4_later = tie(far0, w4)
    z_set = [w0, w1_later, w2_later, w3_later, w4_later]
    state = attend(((-1, 0, 1024),), *common, (up,), (mark, state[1]), False, 10)
    state = attend(((1, 0, 1024),), *common, (down,), state, False, 14)
    mark, x2 = tie(state[0], x2)
    state = (mark, state[1])
    x_set = [x0, x1, x2, x3, x4]
    weights = []
    for values in (z_set, x_set):
        weights += values + [between_cores(v) for v in values[1:4]]
    out = attend(((-2, 0, 512), (2, 512, 512)), *common, (far0, far1), state, True, 7)

    pieces = out.reshape(GROUP, ROWS, 256)
    attended = [lax.dynamic_index_in_dim(pieces, group, 0, keepdims=False)]
    for r in (1, 2, 3):
        sent = lax.dynamic_index_in_dim(pieces, group ^ r, 0, keepdims=False)
        attended.append(swap(sent, ("xh", "c"), r, 4))
    resid, gated = glu(attended, local, ln_conv_gain[None], weights)

    seq = ("y", "xh", "c")
    below = lax.ppermute(gated[ROWS - HALF :], seq, [(i, i + 1) for i in range(15)])
    above = lax.ppermute(gated[:HALF], seq, [(i + 1, i) for i in range(15)])
    frame = first_frame + jnp.arange(ROWS, dtype=jnp.int32)
    begin, end = spans(frame)
    taps = jnp.stack([begin - frame + HALF, end - frame + HALF], 0)
    blocks = slice(0, None, RB), slice(RB - 1, None, RB)
    plain = jnp.logical_and(
        begin[blocks[1]] <= frame[blocks[0]] - HALF, end[blocks[0]] >= frame[blocks[1]] + HALF
    ).astype(jnp.int32)
    taps = jnp.broadcast_to(taps[:, :, None], (2, ROWS, 128))
    dw = jnp.transpose(dw_kernel.reshape(CONV_K, TILES, 128), (1, 0, 2))
    rest = (taps, dw, ln_mid_gain[None], resid)
    inner = conv_inner(plain, gated, *rest)
    return conv_edges(plain, inner, gated, below, above, *rest)[None]


def solution(mesh):
    fine = Mesh(mesh.devices.reshape(8, 2, 4, 2, 2), ("z", "xl", "y", "xh", "c"))
    dp, seq = ("z", "xl"), ("y", "xh", "c")
    return jax.shard_map(
        body,
        mesh=fine,
        in_specs=(
            P(dp, seq, None),
            P(dp, seq),
            P(),
            P(dp, None),
            P(dp, None),
            P(),
            P(dp, None),
            P(),
            P(),
        ),
        out_specs=P(dp, seq, None),
        check_vma=False,
    )
```
